512 devices in a mesh: dp: 4 (over x), expert: 128 (over z, y, core).
Axes of the slice: x: 4, y: 8, z: 8, core: 2. Of those that a mesh axis runs over, the one named last changes fastest.
Arguments:
- tokens: bfloat16 [8192, 2048], P(('dp', 'expert')), may hold values from -6 to 6
- routes: int32 [8192, 8], P(('dp', 'expert')), may hold values from 0 to 127, all different within a row; in each aligned block of 16 rows (0 to 15, 16 to 31, ...) at most 2 rows name the same one
- gates: float32 [8192, 8], P(('dp', 'expert')), may hold values from 0.02 to 0.5
- cotangent: bfloat16 [8192, 2048], P(('dp', 'expert')), may hold values from -6 to 6
- w_gate: bfloat16 [128, 2048, 768], P('expert', 'dp'), may hold values from -0.125 to 0.125
- w_up: bfloat16 [128, 2048, 768], P('expert', 'dp'), may hold values from -0.125 to 0.125
- w_down: bfloat16 [128, 768, 2048], P('expert', None, 'dp'), may hold values from -0.21875 to 0.21875
Outputs:
- layer_out: bfloat16 [8192, 2048], P(('dp', 'expert'))
- d_tokens: bfloat16 [8192, 2048], P(('dp', 'expert'))
- grad_gate: bfloat16 [128, 2048, 768], P('expert', 'dp')
- grad_up: bfloat16 [128, 2048, 768], P('expert', 'dp')
- grad_down: bfloat16 [128, 768, 2048], P('expert', None, 'dp')
The draws below stay inside these ranges and needn't reach their ends.
Inputs may be any that keep to these rules, and one draw needn't show every extreme that they name: `routes`: each token names 8 different experts. Among the 16 tokens of one device (aligned blocks of token rows) no expert is named by more than 2 tokens, a bound that some block reaches.
All inputs are finite; a program needn't handle non-finite values.
Results may differ from the reference program's by a relative error of at most 0.019.
Values may be sent and summed in bfloat16 or wider, within the bound.
A program may use at most 64 MiB of HBM per device.

```python
import math
import jax
import jax.numpy as jnp
import numpy as np
from jax import lax

D = 2048
FF = 768
TOP = 8
TOK_DEV = 16
EXPERTS = 128
CAP = 2
DQ = 512
TOKENS = 8192
N_DP = 4


def block_levels(own_key, extent, shards, least, top_value):
    loudness, own = 1.0, jax.random.fold_in(own_key, 6)
    for dim, blocks in shards:
        steps = jnp.exp(jax.random.uniform(jax.random.fold_in(own, dim), (blocks,), jnp.float32, least / len(shards), top_value / len(shards)))
        loudness = loudness * jnp.repeat(steps, extent[dim] // blocks).reshape([-1 if axis == dim else 1 for axis in range(len(extent))])
    return loudness


def shared_out(own_key, own, number, rows, count, top, limit, lean):
    order = jax.random.permutation(own_key, count)
    heavy_load, common = portions_of(count, rows * top, limit, lean, True), portions_of(count, rows * top, limit, lean, False)
    places = jnp.arange(count)

    def named(tallies, turn):
        used = int((tallies > 0).sum())
        fixed = max(1, used // 4)
        moved = fixed + (places - fixed + turn * (used - fixed)) % max(1, count - fixed)
        return jnp.zeros((count,), jnp.int32).at[order[jnp.where(places < fixed, places, moved)]].set(jnp.asarray(tallies, jnp.int32))

    tallies = jnp.where(number % 4 == 0, named(heavy_load, number // 4), named(common, number - number // 4 - 1))
    mixed = jax.random.permutation(jax.random.fold_in(own, 3), count)
    giver, taker = mixed[0:count // 2 * 2:2], mixed[1:count // 2 * 2:2]
    slack = jnp.minimum(tallies[giver] - 1, limit - tallies[taker]) // 2
    slack = jnp.where((giver == order[0]) | (taker == order[0]) | (tallies[taker] == 0), 0, jnp.maximum(slack, 0))
    moved = jax.random.randint(jax.random.fold_in(own, 4), (count // 2,), 0, 1 << 20) % (slack + 1)
    tallies = tallies.at[giver].add(-moved).at[taker].add(moved)
    members = jnp.searchsorted(jnp.cumsum(tallies), jnp.arange(rows * top), side="right").astype(jnp.int32)
    table = members.reshape(top, rows).T
    table = table[jax.random.permutation(jax.random.fold_in(own, 1), rows)]
    turn = jax.random.randint(jax.random.fold_in(own, 2), (rows, 1), 0, top)
    return jnp.take_along_axis(table, (jnp.arange(top)[None, :] + turn) % top, axis=1)


def portions_of(count, total, most, lean, full):
    weights = [(1 << 20) // math.isqrt(grade ** lean) + 1 for grade in range(1, count + 1)]
    largest = most if full else min(most, max(-(-total // count), total * weights[0] // sum(weights)))
    least = 1 if total - largest >= count - 1 else 0
    holding, surplus = [largest] + [least] * (count - 1), total - largest - least * (count - 1)
    while surplus > 0:
        free = [i for i in range(1, count) if holding[i] < largest] or [i for i in range(1, count) if holding[i] < most]
        pool, left = sum([weights[i] for i in free]), surplus
        for i in free:
            addition = min(most - holding[i], max(1, left * weights[i] // pool), surplus)
            holding[i] = holding[i] + addition
            surplus = surplus - addition
    return np.array(holding)


def noise(key, dims, width, bound, shards=(), held_as=jnp.bfloat16):
    values = width * jax.random.normal(key, dims, jnp.float32)
    if shards:
        values = values * block_levels(key, dims, shards, -0.22, 0.18)
    return jnp.clip(values, -bound, bound).astype(held_as)


def setup_inputs(seed: int = 0) -> dict:
    streams_of = jax.random.split(jax.random.key(seed), 8)
    tokens = noise(streams_of[0], (TOKENS, D), 1.0, 6.0, ((0, 512),))
    routes_keys = jax.random.split(jax.random.fold_in(streams_of[1], 1), TOKENS // TOK_DEV)
    routes_turns = jax.random.permutation(jax.random.fold_in(streams_of[1], 3), TOKENS // TOK_DEV)
    routes = jax.vmap(lambda own, number: shared_out(jax.random.fold_in(streams_of[1], 2), own, number, TOK_DEV, EXPERTS, TOP, CAP, 2))(routes_keys, routes_turns).reshape((TOKENS, TOP))
    gates = jnp.clip(jnp.exp(math.log(0.5) - 3.218876 * jax.random.uniform(streams_of[2], (TOKENS, TOP), jnp.float32) ** block_levels(streams_of[2], (TOKENS, TOP), ((0, 512),), -0.2, 0.2)), 0.02, 0.5)
    cotangent = noise(streams_of[3], (TOKENS, D), 1.0, 6.0, ((0, 512),))
    w_gate = noise(streams_of[4], (EXPERTS, D, FF), D ** -0.5, 0.125, ((0, 128), (1, 4)))
    w_up = noise(streams_of[5], (EXPERTS, D, FF), D ** -0.5, 0.125, ((0, 128), (1, 4)))
    w_down = noise(streams_of[6], (EXPERTS, FF, D), FF ** -0.5, 0.21875, ((0, 128), (2, 4)))
    return {"tokens": tokens, "routes": routes, "gates": gates, "cotangent": cotangent, "w_gate": w_gate, "w_up": w_up, "w_down": w_down}


def part_sum(left, weight_parts, form):
    pieces = jnp.einsum(form, left, weight_parts)
    pieces = lax.optimization_barrier(pieces.astype(jnp.bfloat16))
    return jnp.sum(pieces.astype(jnp.float32), axis=0)


def reference(tokens, routes, gates, cotangent, w_gate, w_up, w_down):
    sources = TOKENS // TOK_DEV
    assigned = TOK_DEV * TOP
    slot_rows = sources * CAP
    expert_ids = routes.reshape(sources, assigned)
    expert_iota = jnp.arange(EXPERTS, dtype=jnp.int32)
    onehot = (expert_ids[:, :, None] == expert_iota[None, None, :]).astype(jnp.int32)
    prior_count = jnp.cumsum(onehot, axis=1) - onehot
    slot_index = jnp.sum(prior_count * onehot, axis=2).astype(jnp.int32)
    source_iota = jnp.arange(sources, dtype=jnp.int32)[:, None]
    flat_pos = (expert_ids * slot_rows + source_iota * CAP + slot_index).reshape(-1)
    labels = (jnp.arange(sources * assigned, dtype=jnp.int32) + 1).astype(jnp.int32)
    table = jnp.zeros((EXPERTS * slot_rows,), jnp.int32).at[flat_pos].set(labels)
    table = table.reshape(EXPERTS, slot_rows)
    gate_flat = gates.reshape(-1)

    def per_expert(carry, inputs):
        out_acc, grad_acc = carry
        labels_here, gate_w, up_w, down_w = inputs
        valid = labels_here > 0
        assign_index = jnp.maximum(labels_here - 1, 0).astype(jnp.int32)
        token_index = (assign_index // TOP).astype(jnp.int32)
        input_rows = jnp.where(valid[:, None], tokens[token_index], jnp.zeros((), jnp.bfloat16)).astype(jnp.bfloat16)
        gate_rows = jnp.where(valid, gate_flat[assign_index], jnp.zeros((), jnp.float32))
        dout_rows = (gate_rows[:, None] * cotangent[token_index].astype(jnp.float32)).astype(jnp.bfloat16)
        left_parts = input_rows.astype(jnp.float32).reshape(slot_rows, N_DP, DQ)
        gate_pre = part_sum(left_parts, gate_w.astype(jnp.float32).reshape(N_DP, DQ, FF), "rqd,qdf->qrf")
        up_pre = part_sum(left_parts, up_w.astype(jnp.float32).reshape(N_DP, DQ, FF), "rqd,qdf->qrf")
        sigmoid_gate = jax.nn.sigmoid(gate_pre)
        silu_gate = gate_pre * sigmoid_gate
        hidden = (silu_gate * up_pre).astype(jnp.bfloat16)
        expert_out = jnp.dot(hidden, down_w, preferred_element_type=jnp.float32).astype(jnp.bfloat16)
        dout_parts = dout_rows.astype(jnp.float32).reshape(slot_rows, N_DP, DQ)
        d_hidden = part_sum(dout_parts, down_w.astype(jnp.float32).reshape(FF, N_DP, DQ), "rqd,fqd->qrf")
        d_gate_pre = (d_hidden * up_pre * sigmoid_gate * (1.0 + gate_pre * (1.0 - sigmoid_gate))).astype(jnp.bfloat16)
        d_up_pre = (d_hidden * silu_gate).astype(jnp.bfloat16)
        grad_down = jnp.einsum("rf,rd->fd", hidden.astype(jnp.float32), dout_rows.astype(jnp.float32)).astype(jnp.bfloat16)
        grad_gate = jnp.einsum("rd,rf->df", input_rows.astype(jnp.float32), d_gate_pre.astype(jnp.float32)).astype(jnp.bfloat16)
        grad_up = jnp.einsum("rd,rf->df", input_rows.astype(jnp.float32), d_up_pre.astype(jnp.float32)).astype(jnp.bfloat16)
        d_assign = (jnp.einsum("rf,df->rd", d_gate_pre.astype(jnp.float32), gate_w.astype(jnp.float32))
                    + jnp.einsum("rf,df->rd", d_up_pre.astype(jnp.float32), up_w.astype(jnp.float32))).astype(jnp.bfloat16)
        out_terms = jnp.where(valid[:, None], gate_rows[:, None] * expert_out.astype(jnp.float32), jnp.zeros((), jnp.float32))
        grad_terms = jnp.where(valid[:, None], d_assign.astype(jnp.float32), jnp.zeros((), jnp.float32))
        out_acc = out_acc.at[token_index].add(out_terms)
        grad_acc = grad_acc.at[token_index].add(grad_terms)
        return (out_acc, grad_acc), (grad_gate, grad_up, grad_down)

    start = (jnp.zeros((TOKENS, D), jnp.float32), jnp.zeros((TOKENS, D), jnp.float32))
    (out_acc, grad_acc), (grad_gate, grad_up, grad_down) = lax.scan(per_expert, start, (table, w_gate, w_up, w_down))
    return out_acc.astype(jnp.bfloat16), grad_acc.astype(jnp.bfloat16), grad_gate, grad_up, grad_down
```

```python
import functools

import jax
import jax.numpy as jnp
from jax import lax
from jax.experimental import pallas as pl
from jax.experimental.pallas import tpu as pltpu
from jax.sharding import PartitionSpec as P

MESH = pl.DeviceIdType.MESH
LAYOUT = {128: (8, 8, 2), 4: (2, 2, 1), 8: (2, 2, 2)}
F32, BF16 = jnp.float32, jnp.bfloat16


def fit(total, want):
    return want if total % want == 0 else total


class Sems:
    def __init__(self):
        self.count = 0

    def take(self, n):
        first = self.count
        self.count += n
        return first


def body(
    cfg,
    routes_ref, gates_ref, tok_ref, cot_ref, wg_hbm, wu_hbm, wd_hbm,
    out_ref, dtok_ref, gg_ref, gu_ref, gd_ref,
    wgu, wd, xinfo, xdata, ginfo, gdata, dmat, whi, wlo, gcol,
    rows, recv, pgu, pdh, rgu, rdh, hid, dgu, gate_s, gacc, gdacc,
    ret_s, ret, part, psum, fin, land,
    wsem, ssem, rsem,
):
    nz, ny, nc, dq, ff, tok = cfg
    xs = 4
    i = lax.axis_index("dp")
    e = lax.axis_index("expert")
    z, yc = e // (ny * nc), e % (ny * nc)
    y, c = yc // nc, yc % nc
    zc = z * nc + c
    right, left, opp = (i + 1) % xs, (i + 3) % xs, (i + 2) % xs
    sems = Sems()

    nsrc = (nz, ny)
    nq = (ny * nc, nz * nc)
    me_src = (z, y)
    me_q = (yc, zc)

    def src_dev(kind, p):
        return (p * ny + y) * nc + c if kind == 0 else (z * ny + p) * nc + c

    def q_dev(kind, q):
        return z * ny * nc + q if kind == 0 else ((q // nc) * ny + y) * nc + q % nc

    half = (nq[0] * nsrc[0] * 2, nq[1] * nsrc[1] * 2)
    base = (0, half[0])
    total = half[0] + half[1]
    blk = total // xs
    ntok = (nsrc[0] * tok, nsrc[1] * tok)

    def rdma(src, dst, sem, dev):
        return pltpu.make_async_remote_copy(
            src_ref=src, dst_ref=dst, send_sem=ssem.at[sem], recv_sem=rsem.at[sem],
            device_id=dev, device_id_type=MESH,
        )

    started = []

    def wait_recv(ref, sem):
        rdma(ref, ref, sem, (i, e)).wait_recv()

    def note_send(ref, sem):
        started.append((ref, sem))

    loads = [
        pltpu.make_async_copy(wg_hbm.at[0], wgu.at[:, pl.ds(0, ff)], wsem.at[0]),
        pltpu.make_async_copy(wu_hbm.at[0], wgu.at[:, pl.ds(ff, ff)], wsem.at[1]),
        pltpu.make_async_copy(wd_hbm.at[0], wd, wsem.at[2]),
    ]
    for load in loads:
        load.start()

    barrier = pltpu.get_barrier_semaphore()
    for k in range(1, xs):
        pl.semaphore_signal(barrier, inc=1, device_id=((i + k) % xs, e), device_id_type=MESH)
    for kind in range(2):
        @pl.loop(1, nq[kind])
        def _(k, kind=kind):
            peer = q_dev(kind, (me_q[kind] + k) % nq[kind])
            pl.semaphore_signal(barrier, inc=1, device_id=(i, peer), device_id_type=MESH)
    pl.semaphore_wait(barrier, xs - 1 + nq[0] - 1 + nq[1] - 1)

    info_refs = (routes_ref, gates_ref)
    data_refs = (tok_ref, cot_ref)
    x_sems = []
    for t in range(2):
        si, sd = sems.take(1), sems.take(1)
        x_sems.append((si, sd))
        for k in range(1, xs):
            peer = (i + k) % xs
            rdma(info_refs[t], xinfo.at[t, i], si, (peer, e)).start()
            rdma(
                data_refs[t].at[:, pl.ds(pl.multiple_of(peer * dq, 128), dq)],
                xdata.at[t, i], sd, (peer, e),
            ).start()
        xinfo[t, i] = info_refs[t][...]
        xdata[t, i] = data_refs[t][:, pl.ds(pl.multiple_of(i * dq, 128), dq)]
        note_send(xinfo.at[t, pl.ds(0, xs - 1)], si)
        note_send(xdata.at[t, pl.ds(0, xs - 1)], sd)

    g_sems = [[None] * 2 for _ in range(2)]
    d_sems = [[[None] * 2 for _ in range(2)] for _ in range(2)]
    for t in range(2):
        si, sd = x_sems[t]
        wait_recv(xinfo.at[t, pl.ds(0, xs - 1)], si)
        wait_recv(xdata.at[t, pl.ds(0, xs - 1)], sd)
        for kind in range(2):
            g_sems[t][kind] = sems.take(1)
            n = nsrc[kind]

            @pl.loop(1, n)
            def _(k, t=t, kind=kind, n=n):
                p = (me_src[kind] + k) % n
                rdma(
                    xinfo.at[t, pl.ds(2 * kind, 2)], ginfo.at[t, kind, me_src[kind]],
                    g_sems[t][kind], (i, src_dev(kind, p)),
                ).start()
            ginfo[t, kind, me_src[kind]] = xinfo[t, 2 * kind : 2 * kind + 2]
            note_send(ginfo.at[t, kind, pl.ds(0, n - 1)], g_sems[t][kind])
        for s in range(2):
            for kind in range(2):
                d_sems[t][s][kind] = sem = sems.take(1)
                n = nsrc[kind]

                @pl.loop(1, n)
                def _(k, t=t, s=s, kind=kind, n=n, sem=sem):
                    p = (me_src[kind] + k) % n
                    rdma(
                        xdata.at[t, 2 * kind + s],
                        gdata.at[t, s, kind, pl.ds(pl.multiple_of(me_src[kind] * tok, tok), tok)],
                        sem, (i, src_dev(kind, p)),
                    ).start()
                gdata[t, s, kind, pl.ds(pl.multiple_of(me_src[kind] * tok, tok), tok)] = xdata[
                    t, 2 * kind + s
                ]
                note_send(gdata.at[t, s, kind, pl.ds(0, (n - 1) * tok)], sem)

    def q_exchange(src, dst, kind):
        sem = sems.take(1)
        n, size = nq[kind], nsrc[kind] * 2
        mine = pl.ds(pl.multiple_of(base[kind] + me_q[kind] * size, size), size)

        @pl.loop(1, n)
        def _(k):
            q = (me_q[kind] + k) % n
            rdma(
                src.at[pl.ds(pl.multiple_of(base[kind] + q * size, size), size)],
                dst.at[mine], sem, (i, q_dev(kind, q)),
            ).start()
        dst[mine] = src[mine]
        view = dst.at[pl.ds(base[kind], (n - 1) * size)]
        note_send(view, sem)
        return view, sem

    lane = lax.broadcasted_iota(jnp.int32, (1, 128), 1) // tok

    def gathered(t, s, kind):
        tile = jnp.zeros((8, 128), F32)
        for p in range(nsrc[kind]):
            tile = jnp.where(lane == p, ginfo[t, kind, p, s], tile)
        return tile

    def matches(kind, s):
        tile = gathered(0, s, kind)
        q = lax.broadcasted_iota(jnp.int32, (nq[kind], 128), 0)
        wanted = q_dev(kind, q).astype(F32)
        return [tile[k : k + 1] == wanted for k in range(8)]

    seg_r = lax.broadcasted_iota(jnp.int32, (128, 128), 0)
    seg_c = lax.broadcasted_iota(jnp.int32, (128, 128), 1)
    earlier = jnp.where((seg_r // tok == seg_c // tok) & (seg_r < seg_c), 1.0, 0.0).astype(BF16)

    for t in range(1):
        for kind in range(2):
            wait_recv(ginfo.at[t, kind, pl.ds(0, nsrc[kind] - 1)], g_sems[t][kind])
    for s in range(2):
        for kind in range(2):
            hit = jnp.zeros((nq[kind], 128), F32)
            for m in matches(kind, s):
                hit = jnp.where(m, 1.0, hit)
            prior = jnp.dot(hit.astype(BF16), earlier, preferred_element_type=F32)
            first = jnp.where(prior < 0.5, hit, 0.0)
            second = hit - first
            size = nsrc[kind] * 2
            r = lax.broadcasted_iota(jnp.int32, (size, 128), 0)
            cell = lax.broadcasted_iota(jnp.int32, (size, 128), 1) // tok == r // 2
            seg0 = jnp.where(cell & (r % 2 == 0), 1.0, 0.0)
            seg1 = jnp.where(cell & (r % 2 == 1), 1.0, 0.0)
            for q in range(nq[kind]):
                dmat[s, pl.ds(base[kind] + q * size, size), :] = (
                    seg0 * first[q : q + 1] + seg1 * second[q : q + 1]
                ).astype(BF16)

    arrivals = [[[None] * 2 for _ in range(2)] for _ in range(2)]

    def send_rows(t, s):
        for kind in range(2):
            wait_recv(gdata.at[t, s, kind, pl.ds(0, (nsrc[kind] - 1) * tok)], d_sems[t][s][kind])
            span = pl.ds(base[kind], half[kind])
            picked = jnp.dot(
                dmat[s, span, : ntok[kind]], gdata[t, s, kind, : ntok[kind]],
                preferred_element_type=F32,
            )
            if t == 1:
                picked = picked * gcol[s, span, :]
            rows[t, s, span, :] = picked.astype(BF16)
            arrivals[t][s][kind] = q_exchange(rows.at[t, s], recv.at[t, s], kind)

    for s in range(2):
        send_rows(0, s)

    for kind in range(2):
        wait_recv(ginfo.at[1, kind, pl.ds(0, nsrc[kind] - 1)], g_sems[1][kind])
    for s in range(2):
        for kind in range(2):
            tile = gathered(1, s, kind)
            gate = jnp.zeros((nq[kind], 128), F32)
            for k, m in enumerate(matches(kind, s)):
                gate = jnp.where(m, tile[k : k + 1], gate)
            size = nsrc[kind] * 2
            for q in range(nq[kind]):
                span = pl.ds(base[kind] + q * size, size)
                w = dmat[s, span, :].astype(F32) * gate[q : q + 1]
                hi = w.astype(BF16)
                whi[s, span, :] = hi
                wlo[s, span, :] = (w - hi.astype(F32)).astype(BF16)
                gcol[s, span, :] = jnp.sum(w, axis=1, keepdims=True)

    for s in range(2):
        send_rows(1, s)

    def chunk(k):
        return pl.ds(pl.multiple_of(k * blk, blk), blk)

    def ring_sum_1(p, r, w):
        sem = sems.take(6)
        a, b = pl.ds(0, w), pl.ds(w, w)
        sends = (
            (p.at[chunk(opp), a], 0, right), (p.at[chunk(opp), b], 1, left),
            (p.at[chunk(left), a], 2, left), (p.at[chunk(right), b], 3, right),
        )
        for src, slot, dev in sends:
            rdma(src, r.at[slot], sem + slot, (dev, e)).start()
            note_send(r.at[slot], sem + slot)
        return sem

    def ring_sum_2(p, r, w, sem):
        for slot, lanes, dev in ((0, pl.ds(0, w), right), (1, pl.ds(w, w), left)):
            wait_recv(r.at[slot], sem + slot)
            r[6 + slot] = (
                r[slot].astype(F32) + p[chunk(dev), lanes].astype(F32)
            ).astype(BF16)
            rdma(r.at[6 + slot], r.at[4 + slot], sem + 4 + slot, (dev, e)).start()
            note_send(r.at[4 + slot], sem + 4 + slot)

    def ring_sum_3(p, r, w, sem):
        for slot in range(2, 6):
            wait_recv(r.at[slot], sem + slot)
        a = p[chunk(i), :w].astype(F32) + r[2].astype(F32) + r[4].astype(F32)
        b = p[chunk(i), w:].astype(F32) + r[3].astype(F32) + r[5].astype(F32)
        return a, b

    def ring_gather_1(g):
        sem = sems.take(4)
        rdma(g.at[chunk(i)], g.at[chunk(i)], sem, (right, e)).start()
        rdma(g.at[chunk(i)], g.at[chunk(i)], sem + 1, (left, e)).start()
        note_send(g.at[chunk(i)], sem)
        note_send(g.at[chunk(i)], sem + 1)
        return sem

    def ring_gather_2(g, w, sem):
        for k, frm, dev in ((0, left, right), (1, right, left)):
            wait_recv(g.at[chunk(frm)], sem + k)
            view = g.at[chunk(frm), pl.ds(k * w, w)]
            rdma(view, view, sem + 2 + k, (dev, e)).start()
            note_send(view, sem + 2 + k)

    def ring_gather_3(g, w, sem):
        for k in range(2):
            wait_recv(g.at[chunk(opp), pl.ds(k * w, w)], sem + 2 + k)

    CONTRACT_LAST = (((1,), (1,)), ((), ()))
    CONTRACT_FIRST = (((0,), (0,)), ((), ()))

    def rows_ready(t, s):
        for kind in range(2):
            view, sem = arrivals[t][s][kind]
            wait_recv(view, sem)

    tn = fit(2 * ff, 256)
    tf = fit(ff, 256)
    td = fit(dq, 256)

    def gate_up(s):
        rows_ready(0, s)

        @pl.loop(0, 2 * ff // tn)
        def _(n):
            cols = pl.ds(pl.multiple_of(n * tn, tn), tn)
            pgu[s, :, cols] = jnp.dot(
                recv[0, s], wgu[:, cols], preferred_element_type=F32
            ).astype(BF16)
        return ring_sum_1(pgu.at[s], rgu.at[s], ff)

    def d_hidden(s):
        rows_ready(1, s)

        @pl.loop(0, ff // tf)
        def _(n):
            cols = pl.ds(pl.multiple_of(n * tf, tf), tf)
            pdh[s, :, cols] = lax.dot_general(
                recv[1, s], wd[cols, :], CONTRACT_LAST, preferred_element_type=F32
            ).astype(BF16)
        return ring_sum_1(pdh.at[s], rdh.at[s], ff // 2)

    def hidden(s, sem):
        gate, up = ring_sum_3(pgu.at[s], rgu.at[s], ff, sem)
        gate_s[s, 0] = gate
        gate_s[s, 1] = up
        hid[s, chunk(i), :] = (gate * jax.nn.sigmoid(gate) * up).astype(BF16)
        return ring_gather_1(hid.at[s])

    def d_gate_up(s, sem):
        w = ff // 2
        parts = ring_sum_3(pdh.at[s], rdh.at[s], w, sem)
        for k in range(2):
            cols = slice(k * w, (k + 1) * w)
            gate, up, dh = gate_s[s, 0, :, cols], gate_s[s, 1, :, cols], parts[k]
            sig = jax.nn.sigmoid(gate)
            dgu[s, chunk(i), pl.ds(k * w, w)] = (
                dh * up * sig * (1.0 + gate * (1.0 - sig))
            ).astype(BF16)
            dgu[s, chunk(i), pl.ds(ff + k * w, w)] = (dh * (gate * sig)).astype(BF16)
        return ring_gather_1(dgu.at[s])

    def out_rows(s):
        @pl.loop(0, dq // td)
        def _(n):
            cols = pl.ds(pl.multiple_of(n * td, td), td)
            ret_s[0, s, :, cols] = jnp.dot(
                hid[s], wd[:, cols], preferred_element_type=F32
            ).astype(BF16)
        return [q_exchange(ret_s.at[0, s], ret.at[0, s], kind) for kind in range(2)]

    def back_rows(s):
        @pl.loop(0, dq // td)
        def _(n):
            cols = pl.ds(pl.multiple_of(n * td, td), td)
            ret_s[1, s, :, cols] = lax.dot_general(
                dgu[s], wgu[cols, :], CONTRACT_LAST, preferred_element_type=F32
            ).astype(BF16)
        return [q_exchange(ret_s.at[1, s], ret.at[1, s], kind) for kind in range(2)]

    def combine(t, s, arrived):
        result = []
        for kind in range(2):
            wait_recv(*arrived[kind])
            span = pl.ds(base[kind], half[kind])
            got = ret[t, s, span, :]
            if t == 0:
                sums = lax.dot_general(
                    whi[s, span, :], got, CONTRACT_FIRST, preferred_element_type=F32
                ) + lax.dot_general(
                    wlo[s, span, :], got, CONTRACT_FIRST, preferred_element_type=F32
                )
            else:
                sums = lax.dot_general(
                    dmat[s, span, :], got, CONTRACT_FIRST, preferred_element_type=F32
                )
            part[t, s, kind] = sums[: ntok[kind]].astype(BF16)
            sem = sems.take(1)
            n = nsrc[kind]
            mine = pl.ds(pl.multiple_of(me_src[kind] * tok, tok), tok)

            @pl.loop(1, n)
            def _(k, kind=kind, n=n, sem=sem, mine=mine):
                p = (me_src[kind] + k) % n
                rdma(
                    part.at[t, s, kind, pl.ds(pl.multiple_of(p * tok, tok), tok)],
                    psum.at[t, s, kind, mine], sem, (i, src_dev(kind, p)),
                ).start()
            psum[t, s, kind, mine] = part[t, s, kind, mine]
            view = psum.at[t, s, kind, pl.ds(0, (n - 1) * tok)]
            note_send(view, sem)
            result.append((view, sem))
        return result

    def finish(t, s, arrived):
        for kind in range(2):
            wait_recv(*arrived[kind])
            acc = psum[t, s, kind, :tok].astype(F32)
            for p in range(1, nsrc[kind]):
                acc = acc + psum[t, s, kind, p * tok : (p + 1) * tok].astype(F32)
            fin[t, 2 * kind + s] = acc.astype(BF16)

    def give_back(t):
        sem = sems.take(1)
        lanes = pl.ds(pl.multiple_of(i * dq, 128), dq)
        for k in range(1, xs):
            peer = (i + k) % xs
            rdma(fin.at[t, peer], land.at[t, i], sem, (peer, e)).start()
        land[t, i] = fin[t, i]
        view = land.at[t, pl.ds(0, xs - 1)]
        note_send(view, sem)
        return view, sem

    def grad_down(s):
        @pl.loop(0, ff // tf)
        def _(n):
            cols = pl.ds(pl.multiple_of(n * tf, tf), tf)
            value = lax.dot_general(
                hid[s, :, cols], recv[1, s], CONTRACT_FIRST, preferred_element_type=F32
            )
            if s == 0:
                gdacc[cols, :] = value
            else:
                gd_ref[0, cols, :] = (gdacc[cols, :] + value).astype(BF16)

    def grad_gate_up(s):
        for k, ref in ((0, gg_ref), (1, gu_ref)):
            @pl.loop(0, ff // tf)
            def _(n, k=k, ref=ref):
                cols = pl.ds(pl.multiple_of(n * tf, tf), tf)
                both = pl.ds(pl.multiple_of(k * ff + n * tf, tf), tf)
                value = lax.dot_general(
                    recv[0, s], dgu[s, :, both], CONTRACT_FIRST, preferred_element_type=F32
                )
                if s == 0:
                    gacc[:, both] = value
                else:
                    ref[0, :, cols] = (gacc[:, both] + value).astype(BF16)

    loads[0].wait()
    loads[1].wait()
    gu0 = gate_up(0)
    gu1 = gate_up(1)
    ring_sum_2(pgu.at[0], rgu.at[0], ff, gu0)
    loads[2].wait()
    dh0 = d_hidden(0)
    ring_sum_2(pgu.at[1], rgu.at[1], ff, gu1)
    dh1 = d_hidden(1)
    h0 = hidden(0, gu0)
    ring_sum_2(pdh.at[0], rdh.at[0], ff // 2, dh0)
    h1 = hidden(1, gu1)
    ring_sum_2(pdh.at[1], rdh.at[1], ff // 2, dh1)
    g0 = d_gate_up(0, dh0)
    ring_gather_2(hid.at[0], ff // 2, h0)
    g1 = d_gate_up(1, dh1)
    ring_gather_2(hid.at[1], ff // 2, h1)
    ring_gather_3(hid.at[0], ff // 2, h0)
    o0 = out_rows(0)
    grad_down(0)
    ring_gather_2(dgu.at[0], ff, g0)
    ring_gather_3(hid.at[1], ff // 2, h1)
    o1 = out_rows(1)
    ring_gather_2(dgu.at[1], ff, g1)
    co0 = combine(0, 0, o0)
    grad_down(1)
    ring_gather_3(dgu.at[0], ff, g0)
    b0 = back_rows(0)
    co1 = combine(0, 1, o1)
    grad_gate_up(0)
    ring_gather_3(dgu.at[1], ff, g1)
    b1 = back_rows(1)
    finish(0, 0, co0)
    finish(0, 1, co1)
    land_o = give_back(0)
    cb0 = combine(1, 0, b0)
    grad_gate_up(1)
    cb1 = combine(1, 1, b1)
    wait_recv(*land_o)
    for j in range(xs):
        out_ref[:, j * dq : (j + 1) * dq] = land[0, j]
    finish(1, 0, cb0)
    finish(1, 1, cb1)
    land_b = give_back(1)
    wait_recv(*land_b)
    for j in range(xs):
        dtok_ref[:, j * dq : (j + 1) * dq] = land[1, j]
    for ref, sem in started:
        rdma(ref, ref, sem, (i, e)).wait_send()
    assert sems.count <= ssem.shape[0]


def local(shape, tokens, routes, gates, cotangent, w_gate, w_up, w_down):
    nz, ny, nc = shape
    tok, features = tokens.shape
    fanout = routes.shape[1]
    xs = 4
    dq, ff = w_gate.shape[1], w_gate.shape[2]
    copies = 128 // tok
    spread = lambda v: jnp.tile(v.astype(F32).T, (1, copies))
    half = (ny * nc * nz * 2, nz * nc * ny * 2)
    total = half[0] + half[1]
    blk = total // xs
    most = max(nz, ny)
    gtok = most * tok
    V = pltpu.VMEM
    nsem = 96
    vm = pl.BlockSpec(memory_space=pltpu.VMEM)
    hb = pl.BlockSpec(memory_space=pl.ANY)
    sds = jax.ShapeDtypeStruct
    return pl.pallas_call(
        functools.partial(body, (nz, ny, nc, dq, ff, tok)),
        out_shape=(
            sds((tok, features), BF16), sds((tok, features), BF16),
            sds(w_gate.shape, BF16), sds(w_up.shape, BF16), sds(w_down.shape, BF16),
        ),
        in_specs=[vm, vm, vm, vm, hb, hb, hb],
        out_specs=(vm, vm, vm, vm, vm),
        scratch_shapes=[
            V((dq, 2 * ff), BF16),
            V((ff, dq), BF16),
            V((2, xs, fanout, 128), F32),
            V((2, xs, tok, dq), BF16),
            V((2, 2, most, 2, fanout, 128), F32),
            V((2, 2, 2, gtok, dq), BF16),
            V((2, total, 128), BF16),
            V((2, total, 128), BF16),
            V((2, total, 128), BF16),
            V((2, total, 1), F32),
            V((2, 2, total, dq), BF16),
            V((2, 2, total, dq), BF16),
            V((2, total, 2 * ff), BF16),
            V((2, total, ff), BF16),
            V((2, 8, blk, ff), BF16),
            V((2, 8, blk, ff // 2), BF16),
            V((2, total, ff), BF16),
            V((2, total, 2 * ff), BF16),
            V((2, 2, blk, ff), F32),
            V((dq, 2 * ff), F32),
            V((ff, dq), F32),
            V((2, 2, total, dq), BF16),
            V((2, 2, total, dq), BF16),
            V((2, 2, 2, gtok, dq), BF16),
            V((2, 2, 2, gtok, dq), BF16),
            V((2, xs, tok, dq), BF16),
            V((2, xs, tok, dq), BF16),
            pltpu.SemaphoreType.DMA((3,)),
            pltpu.SemaphoreType.DMA((nsem,)),
            pltpu.SemaphoreType.DMA((nsem,)),
        ],
        compiler_params=pltpu.CompilerParams(
            collective_id=0, has_side_effects=True, vmem_limit_bytes=60 * 1024 * 1024
        ),
        name="moe_layer",
    )(spread(routes), spread(gates), tokens, cotangent, w_gate, w_up, w_down)


def solution(mesh):
    return jax.shard_map(
        functools.partial(local, LAYOUT[mesh.shape["expert"]]),
        mesh=mesh,
        in_specs=(
            P(("dp", "expert"), None),
            P(("dp", "expert"), None),
            P(("dp", "expert"), None),
            P(("dp", "expert"), None),
            P("expert", "dp", None),
            P("expert", "dp", None),
            P("expert", None, "dp"),
        ),
        out_specs=(
            P(("dp", "expert"), None),
            P(("dp", "expert"), None),
            P("expert", "dp", None),
            P("expert", "dp", None),
            P("expert", None, "dp"),
        ),
        check_vma=False,
    )
```

```python
import functools

import jax
import jax.numpy as jnp
from jax import lax
from jax.experimental import pallas as pl
from jax.experimental.pallas import tpu as pltpu
from jax.sharding import PartitionSpec as P

MESH = pl.DeviceIdType.MESH
LAYOUT = {128: (8, 8, 2), 8: (2, 2, 2)}
F32, BF16 = jnp.float32, jnp.bfloat16
CONTRACT_LAST = (((1,), (1,)), ((), ()))
CONTRACT_FIRST = (((0,), (0,)), ((), ()))


def fit(total, want):
    return want if total % want == 0 else total


class Sems:
    def __init__(self):
        self.count = 0

    def take(self, n):
        first = self.count
        self.count += n
        return first


def body(
    cfg,
    routes_ref, gates_ref, tok_ref, cot_ref, wg_hbm, wu_hbm, wd_hbm,
    out_hbm, dtok_hbm, gg_hbm, gu_hbm, gd_hbm,
    raw_r, raw_g, own_r, own_g, wgu, wd, xroutes, xgates, xdata, groutes, ggates, gdata, dmat, whi, wlo, gcol,
    rows, recv, pgu, pdh, rgu, rdh, hid, dgu, gate_s, gacc, gdacc,
    ret_s, ret, part, psum, fin, land, gg, gu, gd, tok_out,
    wsem, osem, ssem, rsem,
):
    n8, nc, dq, ff, tok = cfg
    xs = 4
    nq = n8 * nc
    qc = nq // xs
    size = 2 * n8
    blk = 2 * qc * size
    gt = n8 * tok
    i = lax.axis_index("dp")
    e = lax.axis_index("expert")
    z, yc = e // nq, e % nq
    y, c = yc // nc, yc % nc
    right, left, opp = (i + 1) % xs, (i + 3) % xs, (i + 2) % xs
    sems = Sems()

    me_src = (z, y)
    me_q = (yc, z * nc + c)

    def src_dev(kind, p):
        return (p * n8 + y) * nc + c if kind == 0 else (z * n8 + p) * nc + c

    def q_dev(kind, q):
        return z * nq + q if kind == 0 else ((q // nc) * n8 + y) * nc + q % nc

    def q_rows(kind, q):
        at = (q // qc) * blk + kind * (qc * size) + (q % qc) * size
        return pl.ds(at if isinstance(at, int) else pl.multiple_of(at, size), size)

    def src_rows(kind, p):
        return pl.ds(pl.multiple_of(kind * gt + p * tok, tok), tok)

    def rdma(src, dst, sem, dev):
        return pltpu.make_async_remote_copy(
            src_ref=src, dst_ref=dst, send_sem=ssem.at[sem], recv_sem=rsem.at[sem],
            device_id=dev, device_id_type=MESH,
        )

    started = []

    def wait_recv(ref, sem):
        rdma(ref, ref, sem, (i, e)).wait_recv()

    def note_send(ref, sem):
        started.append((ref, sem))

    part_of = lambda ref, k: ref.at[:, pl.ds(pl.multiple_of(k * dq, 128), dq)]
    owns = [
        pltpu.make_async_copy(routes_ref, raw_r, wsem.at[3]),
        pltpu.make_async_copy(part_of(tok_ref, i), xdata.at[0, i], wsem.at[4]),
        pltpu.make_async_copy(gates_ref, raw_g, wsem.at[5]),
        pltpu.make_async_copy(part_of(cot_ref, i), xdata.at[1, i], wsem.at[6]),
    ]
    for own in owns:
        own.start()
    loads = [
        pltpu.make_async_copy(wg_hbm.at[0], wgu.at[:, pl.ds(0, ff)], wsem.at[0]),
        pltpu.make_async_copy(wu_hbm.at[0], wgu.at[:, pl.ds(ff, ff)], wsem.at[1]),
        pltpu.make_async_copy(wd_hbm.at[0], wd, wsem.at[2]),
    ]
    for load in loads:
        load.start()
    for t, raw, tile_ref in ((0, raw_r, own_r), (1, raw_g, own_g)):
        owns[2 * t].wait()
        value = raw[...]
        blank = jnp.zeros((value.shape[0], 128 - tok), value.dtype)
        tile_ref[...] = jnp.concatenate([value, blank], axis=1)

    with jax.named_scope("h_barrier"):
        barrier = pltpu.get_barrier_semaphore()
        for k in range(1, xs):
            pl.semaphore_signal(barrier, inc=1, device_id=((i + k) % xs, e), device_id_type=MESH)
        for kind in range(2):
            @pl.loop(1, nq)
            def _(k, kind=kind):
                peer = q_dev(kind, (me_q[kind] + k) % nq)
                pl.semaphore_signal(barrier, inc=1, device_id=(i, peer), device_id_type=MESH)
        pl.semaphore_wait(barrier, xs - 1 + 2 * (nq - 1))

    info = ((own_r, xroutes, groutes), (own_g, xgates, ggates))
    data_refs = (tok_ref, cot_ref)
    x_sems = []
    with jax.named_scope("h_x"):
        for t in range(2):
            own, xinfo, _ = info[t]
            si, sd = sems.take(1), sems.take(1)
            x_sems.append((si, sd))
            for k in (2, 1, 3):
                peer = (i + k) % xs
                rdma(own, xinfo.at[i], si, (peer, e)).start()
                rdma(part_of(data_refs[t], peer), xdata.at[t, i], sd, (peer, e)).start()
            xinfo[i] = own[...]
            note_send(xinfo.at[pl.ds(0, xs - 1)], si)
            note_send(xdata.at[t, pl.ds(0, xs - 1)], sd)

    def gather_info(t):
        _, xinfo, ginfo = info[t]
        wait_recv(xinfo.at[pl.ds(0, xs - 1)], x_sems[t][0])
        sem = sems.take(1)
        for kind in range(2):
            @pl.loop(1, n8)
            def _(k, kind=kind, sem=sem):
                rdma(
                    xinfo.at[pl.ds(2 * kind, 2)], ginfo.at[kind, me_src[kind]],
                    sem, (i, src_dev(kind, (me_src[kind] + k) % n8)),
                ).start()
            ginfo[kind, me_src[kind]] = xinfo[2 * kind : 2 * kind + 2]
        view = ginfo.at[:, pl.ds(0, n8 - 1)]
        note_send(view, sem)
        return [(view, sem)]

    def gather_data(t, s):
        sem = sems.take(1)
        for kind in range(2):
            @pl.loop(1, n8)
            def _(k, kind=kind, sem=sem):
                rdma(
                    xdata.at[t, 2 * kind + s], gdata.at[t, s, src_rows(kind, me_src[kind])],
                    sem, (i, src_dev(kind, (me_src[kind] + k) % n8)),
                ).start()
            gdata[t, s, src_rows(kind, me_src[kind])] = xdata[t, 2 * kind + s]
        view = gdata.at[t, s, pl.ds(0, 2 * (n8 - 1) * tok)]
        note_send(view, sem)
        return [(view, sem)]

    def wait_all(pairs):
        for view, sem in pairs:
            wait_recv(view, sem)

    def exchange(src, dst):
        sem = sems.take(1)
        for kind in range(2):
            mine = q_rows(kind, me_q[kind])

            @pl.loop(1, nq)
            def _(k, kind=kind, sem=sem, mine=mine):
                q = (me_q[kind] + k) % nq
                rdma(src.at[q_rows(kind, q)], dst.at[mine], sem, (i, q_dev(kind, q))).start()
            dst[mine] = src[mine]
        view = dst.at[pl.ds(0, 2 * (nq - 1) * size)]
        note_send(view, sem)
        return [(view, sem)]

    def tile(ginfo, s, kind):
        return jnp.concatenate([ginfo[kind, p, s][:, :tok] for p in range(n8)], axis=1)

    def matches(s, kind):
        names = tile(groutes, s, kind)
        wanted = q_dev(kind, lax.broadcasted_iota(jnp.int32, (nq, gt), 0))
        return [names[k : k + 1] == wanted for k in range(names.shape[0])]

    before_r = lax.broadcasted_iota(jnp.int32, (gt, gt), 0)
    before_c = lax.broadcasted_iota(jnp.int32, (gt, gt), 1)
    earlier = jnp.where(
        (before_r // tok == before_c // tok) & (before_r < before_c), 1.0, 0.0
    ).astype(BF16)
    slot_r = lax.broadcasted_iota(jnp.int32, (size, gt), 0)
    cell = lax.broadcasted_iota(jnp.int32, (size, gt), 1) // tok == slot_r // 2
    seg0 = jnp.where(cell & (slot_r % 2 == 0), 1.0, 0.0)
    seg1 = jnp.where(cell & (slot_r % 2 == 1), 1.0, 0.0)

    def selection(s):
        nothing = jnp.zeros((size, gt), BF16)
        for kind in range(2):
            hit = jnp.zeros((nq, gt), F32)
            for m in matches(s, kind):
                hit = jnp.where(m, 1.0, hit)
            prior = jnp.dot(hit.astype(BF16), earlier, preferred_element_type=F32)
            first = jnp.where(prior < 0.5, hit, 0.0)
            second = hit - first
            for q in range(nq):
                dmat[s, q_rows(kind, q), pl.ds(kind * gt, gt)] = (
                    seg0 * first[q : q + 1] + seg1 * second[q : q + 1]
                ).astype(BF16)
                dmat[s, q_rows(kind, q), pl.ds((1 - kind) * gt, gt)] = nothing

    def weighting(s):
        nothing = jnp.zeros((size, gt), BF16)
        for kind in range(2):
            values = tile(ggates, s, kind)
            gate = jnp.zeros((nq, gt), F32)
            for k, m in enumerate(matches(s, kind)):
                gate = jnp.where(m, values[k : k + 1], gate)
            for q in range(nq):
                w = dmat[s, q_rows(kind, q), pl.ds(kind * gt, gt)].astype(F32) * gate[q : q + 1]
                hi = w.astype(BF16)
                whi[s, q_rows(kind, q), pl.ds(kind * gt, gt)] = hi
                wlo[s, q_rows(kind, q), pl.ds(kind * gt, gt)] = (w - hi.astype(F32)).astype(BF16)
                whi[s, q_rows(kind, q), pl.ds((1 - kind) * gt, gt)] = nothing
                wlo[s, q_rows(kind, q), pl.ds((1 - kind) * gt, gt)] = nothing
                gcol[s, q_rows(kind, q), :] = jnp.sum(w, axis=1, keepdims=True)

    def send_rows(t, s, gathered):
        wait_all(gathered)
        picked = jnp.dot(dmat[s], gdata[t, s], preferred_element_type=F32)
        if t == 1:
            picked = picked * gcol[s]
        rows[t, s] = picked.astype(BF16)
        return exchange(rows.at[t, s], recv.at[t, s])

    def chunk(k):
        return pl.ds(pl.multiple_of(k * blk, blk), blk)

    def ring_part(p, r, w, sem, which):
        a, b = pl.ds(0, w), pl.ds(w, w)
        for slot in which:
            at, lanes, dev = (
                (opp, a, right), (opp, b, left), (left, a, left), (right, b, right)
            )[slot]
            rdma(p.at[chunk(at), lanes], r.at[slot], sem + slot, (dev, e)).start()
            note_send(r.at[slot], sem + slot)

    def ring_sum_1(p, r, w):
        sem = sems.take(6)
        ring_part(p, r, w, sem, range(4))
        return sem

    def ring_sum_2(p, r, w, sem):
        for slot, lanes, dev in ((0, pl.ds(0, w), right), (1, pl.ds(w, w), left)):
            wait_recv(r.at[slot], sem + slot)
            r[6 + slot] = (
                r[slot].astype(F32) + p[chunk(dev), lanes].astype(F32)
            ).astype(BF16)
            rdma(r.at[6 + slot], r.at[4 + slot], sem + 4 + slot, (dev, e)).start()
            note_send(r.at[4 + slot], sem + 4 + slot)

    def ring_sum_3(p, r, w, sem):
        for slot in range(2, 6):
            wait_recv(r.at[slot], sem + slot)
        a = p[chunk(i), :w].astype(F32) + r[2].astype(F32) + r[4].astype(F32)
        b = p[chunk(i), w:].astype(F32) + r[3].astype(F32) + r[5].astype(F32)
        return a, b

    def ring_gather_1(g, w, sem, half):
        for k, dev in ((0, right), (1, left)):
            view = g.at[chunk(i), pl.ds((k if half == 0 else 1 - k) * w, w)]
            rdma(view, view, sem + 2 * half + k, (dev, e)).start()
            note_send(view, sem + 2 * half + k)

    def ring_gather_2(g, w, sem):
        for k, frm, dev in ((0, left, right), (1, right, left)):
            view = g.at[chunk(frm), pl.ds(k * w, w)]
            wait_recv(view, sem + k)
            rdma(view, view, sem + 4 + k, (dev, e)).start()
            note_send(view, sem + 4 + k)

    def ring_near(g, w, sem):
        for k, frm in ((0, left), (1, right)):
            wait_recv(g.at[chunk(frm), pl.ds((1 - k) * w, w)], sem + 2 + k)

    def ring_gather_3(g, w, sem):
        for k in range(2):
            wait_recv(g.at[chunk(opp), pl.ds(k * w, w)], sem + 4 + k)

    tn = fit(2 * ff, 256)
    tf = fit(ff, 256)
    td = fit(dq, 256)

    def gate_up_block(s, at):
        @pl.loop(0, 2 * ff // tn)
        def _(n):
            cols = pl.ds(pl.multiple_of(n * tn, tn), tn)
            pgu[s, at, cols] = jnp.dot(
                recv[0, s, at], wgu[:, cols], preferred_element_type=F32
            ).astype(BF16)

    def d_hidden(s):
        @pl.loop(0, ff // tf)
        def _(n):
            cols = pl.ds(pl.multiple_of(n * tf, tf), tf)
            pdh[s, :, cols] = lax.dot_general(
                recv[1, s], wd[cols, :], CONTRACT_LAST, preferred_element_type=F32
            ).astype(BF16)
        return ring_sum_1(pdh.at[s], rdh.at[s], ff // 2)

    def hidden(s, sem):
        gate, up = ring_sum_3(pgu.at[s], rgu.at[s], ff, sem)
        gate_s[s, 0] = gate
        gate_s[s, 1] = up
        hid[s, chunk(i), :] = (gate * jax.nn.sigmoid(gate) * up).astype(BF16)
        sem = sems.take(6)
        ring_gather_1(hid.at[s], ff // 2, sem, 0)
        ring_gather_1(hid.at[s], ff // 2, sem, 1)
        return sem

    def d_gate_up(s, sem):
        w = ff // 2
        parts = ring_sum_3(pdh.at[s], rdh.at[s], w, sem)
        for k in range(2):
            cols = slice(k * w, (k + 1) * w)
            gate, up, dh = gate_s[s, 0, :, cols], gate_s[s, 1, :, cols], parts[k]
            sig = jax.nn.sigmoid(gate)
            dgu[s, chunk(i), pl.ds(k * w, w)] = (
                dh * up * sig * (1.0 + gate * (1.0 - sig))
            ).astype(BF16)
            dgu[s, chunk(i), pl.ds(ff + k * w, w)] = (dh * (gate * sig)).astype(BF16)
        return sems.take(6)

    def out_rows(s):
        @pl.loop(0, dq // td)
        def _(n):
            cols = pl.ds(pl.multiple_of(n * td, td), td)
            ret_s[0, s, :, cols] = jnp.dot(
                hid[s], wd[:, cols], preferred_element_type=F32
            ).astype(BF16)
        return exchange(ret_s.at[0, s], ret.at[0, s])

    def back_block(s, at):
        @pl.loop(0, dq // td)
        def _(n):
            cols = pl.ds(pl.multiple_of(n * td, td), td)
            ret_s[1, s, at, cols] = lax.dot_general(
                dgu[s, at], wgu[cols, :], CONTRACT_LAST, preferred_element_type=F32
            ).astype(BF16)

    def back_rows(s):
        back_block(s, slice(None))
        return exchange(ret_s.at[1, s], ret.at[1, s])

    def back_send(s, k, back_sem):
        back_block(s, chunk(k))
        for kind in range(2):
            @pl.loop(0, qc)
            def _(n, kind=kind):
                q = k * qc + n
                there, mine = q_rows(kind, q), q_rows(kind, me_q[kind])

                @pl.when(q != me_q[kind])
                def _():
                    rdma(
                        ret_s.at[1, s, there], ret.at[1, s, mine],
                        back_sem, (i, q_dev(kind, q)),
                    ).start()

                @pl.when(q == me_q[kind])
                def _():
                    ret[1, s, mine] = ret_s[1, s, mine]

    def combine(t, s, arrived):
        wait_all(arrived)
        got = ret[t, s]
        if t == 0:
            sums = lax.dot_general(
                whi[s], got, CONTRACT_FIRST, preferred_element_type=F32
            ) + lax.dot_general(wlo[s], got, CONTRACT_FIRST, preferred_element_type=F32)
        else:
            sums = lax.dot_general(dmat[s], got, CONTRACT_FIRST, preferred_element_type=F32)
        part[t, s] = sums.astype(BF16)
        sem = sems.take(1)
        for kind in range(2):
            mine = src_rows(kind, me_src[kind])

            @pl.loop(1, n8)
            def _(k, kind=kind, sem=sem, mine=mine):
                p = (me_src[kind] + k) % n8
                rdma(
                    part.at[t, s, src_rows(kind, p)], psum.at[t, s, mine],
                    sem, (i, src_dev(kind, p)),
                ).start()
            psum[t, s, mine] = part[t, s, mine]
        view = psum.at[t, s, pl.ds(0, 2 * (n8 - 1) * tok)]
        note_send(view, sem)
        return [(view, sem)]

    def finish(t, s, arrived):
        wait_all(arrived)
        for kind in range(2):
            acc = psum[t, s, kind * gt : kind * gt + tok].astype(F32)
            for p in range(1, n8):
                acc = acc + psum[t, s, kind * gt + p * tok : kind * gt + (p + 1) * tok].astype(F32)
            fin[t, 2 * kind + s] = acc.astype(BF16)

    def give_back(t):
        sem = sems.take(1)
        for k in (2, 1, 3):
            peer = (i + k) % xs
            rdma(fin.at[t, peer], land.at[t, i], sem, (peer, e)).start()
        land[t, i] = fin[t, i]
        view = land.at[t, pl.ds(0, xs - 1)]
        note_send(view, sem)
        return view, sem

    stores = []

    def store(src, dst):
        copy = pltpu.make_async_copy(src, dst, osem.at[len(stores)])
        copy.start()
        stores.append(copy)

    def take_back(t, landed, dst):
        wait_recv(*landed)
        for j in range(xs):
            tok_out[t, :, j * dq : (j + 1) * dq] = land[t, j]
        store(tok_out.at[t], dst)

    def grad_down(s):
        @pl.loop(0, ff // tf)
        def _(n):
            cols = pl.ds(pl.multiple_of(n * tf, tf), tf)
            value = lax.dot_general(
                hid[s, :, cols], recv[1, s], CONTRACT_FIRST, preferred_element_type=F32
            )
            if s == 0:
                gdacc[cols, :] = value
            else:
                gd[cols, :] = (gdacc[cols, :] + value).astype(BF16)
        if s == 1:
            store(gd, gd_hbm.at[0])

    def grad_gate_up(s):
        for k, ref, dst in ((0, gg, gg_hbm), (1, gu, gu_hbm)):
            @pl.loop(0, ff // tf)
            def _(n, k=k, ref=ref):
                cols = pl.ds(pl.multiple_of(n * tf, tf), tf)
                both = pl.ds(pl.multiple_of(k * ff + n * tf, tf), tf)
                value = lax.dot_general(
                    recv[0, s], dgu[s, :, both], CONTRACT_FIRST, preferred_element_type=F32
                )
                if s == 0:
                    gacc[:, both] = value
                else:
                    ref[:, cols] = (gacc[:, both] + value).astype(BF16)
            if s == 1:
                store(ref, dst.at[0])

    step = jax.named_scope
    with step("h_wx0"):
        gi0 = gather_info(0)
        wait_recv(xdata.at[0, pl.ds(0, xs - 1)], x_sems[0][1])
        owns[1].wait()
        t0 = gather_data(0, 0)
        t1 = gather_data(0, 1)
    with step("h_sel0"):
        wait_all(gi0)
        selection(0)
    with step("h_rows0"):
        r0 = send_rows(0, 0, t0)
    with step("h_sel1"):
        selection(1)
    with step("h_rows1"):
        r1 = send_rows(0, 1, t1)
    with step("h_wx1"):
        gi1 = gather_info(1)
        wait_recv(xdata.at[1, pl.ds(0, xs - 1)], x_sems[1][1])
        owns[3].wait()
        c0 = gather_data(1, 0)
        c1 = gather_data(1, 1)
    with step("h_wload"):
        loads[0].wait()
        loads[1].wait()
    with step("a_wrow0"):
        wait_all(r0)
    with step("a_gu0"):
        gu_sem = [sems.take(6), sems.take(6)]
        gate_up_block(0, chunk(opp))
        ring_part(pgu.at[0], rgu.at[0], ff, gu_sem[0], (0, 1))
        gate_up_block(0, chunk(left))
        ring_part(pgu.at[0], rgu.at[0], ff, gu_sem[0], (2,))
        gate_up_block(0, chunk(right))
        ring_part(pgu.at[0], rgu.at[0], ff, gu_sem[0], (3,))
        gate_up_block(0, chunk(i))
    with step("a_wrow1"):
        wait_all(r1)
    with step("a_gu1"):
        gate_up_block(1, slice(None))
    with step("a_gu0r2"):
        ring_sum_2(pgu.at[0], rgu.at[0], ff, gu_sem[0])
        ring_part(pgu.at[1], rgu.at[1], ff, gu_sem[1], range(4))
    with step("h_wei"):
        wait_all(gi1)
        weighting(0)
        weighting(1)
    with step("h_dr0"):
        d0 = send_rows(1, 0, c0)
    with step("h_dr1"):
        d1 = send_rows(1, 1, c1)
        loads[2].wait()
    with step("a_hid0"):
        h0 = hidden(0, gu_sem[0])
    with step("a_dh0"):
        wait_all(d0)
        dh0 = d_hidden(0)
    with step("a_gu1r2"):
        ring_sum_2(pgu.at[1], rgu.at[1], ff, gu_sem[1])
    with step("a_dh1"):
        wait_all(d1)
        dh1 = d_hidden(1)
    with step("a_hg0"):
        ring_gather_2(hid.at[0], ff // 2, h0)
    with step("a_hid1"):
        h1 = hidden(1, gu_sem[1])
    with step("a_dh0r2"):
        ring_sum_2(pdh.at[0], rdh.at[0], ff // 2, dh0)
    with step("a_dh1r2"):
        ring_sum_2(pdh.at[1], rdh.at[1], ff // 2, dh1)
    with step("a_out0"):
        ring_near(hid.at[0], ff // 2, h0)
        ring_gather_3(hid.at[0], ff // 2, h0)
        o0 = out_rows(0)
    with step("a_hg1"):
        ring_gather_2(hid.at[1], ff // 2, h1)
    with step("a_dg0"):
        g0 = d_gate_up(0, dh0)
        ring_gather_1(dgu.at[0], ff, g0, 0)
        ring_gather_1(dgu.at[0], ff, g0, 1)
    with step("a_co0"):
        co0 = combine(0, 0, o0)
    with step("a_dg1"):
        g1 = d_gate_up(1, dh1)
    with step("a_wh1"):
        ring_near(hid.at[1], ff // 2, h1)
        ring_gather_3(hid.at[1], ff // 2, h1)
    with step("a_out1"):
        o1 = out_rows(1)
    with step("a_gg0r2"):
        ring_gather_2(dgu.at[0], ff, g0)
        ring_gather_1(dgu.at[1], ff, g1, 0)
        ring_gather_1(dgu.at[1], ff, g1, 1)
    with step("a_gd0"):
        grad_down(0)
    with step("a_gd1"):
        grad_down(1)
    with step("a_fin00"):
        finish(0, 0, co0)
    with step("a_co1"):
        co1 = combine(0, 1, o1)
    with step("a_wg0"):
        ring_near(dgu.at[0], ff, g0)
        ring_gather_3(dgu.at[0], ff, g0)
    with step("a_back0"):
        b0 = back_rows(0)
    with step("a_gg1r2"):
        ring_gather_2(dgu.at[1], ff, g1)
    back_sem = sems.take(1)
    with step("t_bk1own"):
        back_send(1, i, back_sem)
    with step("t_fin01"):
        finish(0, 1, co1)
        land_o = give_back(0)
    with step("t_wnear"):
        ring_near(dgu.at[1], ff, g1)
    with step("t_bk1lr"):
        back_send(1, left, back_sem)
        back_send(1, right, back_sem)
    with step("t_wlast"):
        ring_gather_3(dgu.at[1], ff, g1)
    with step("t_bk1opp"):
        back_send(1, opp, back_sem)
        view = ret.at[1, 1, pl.ds(0, 2 * (nq - 1) * size)]
        note_send(view, back_sem)
        b1 = [(view, back_sem)]
    with step("t_cb0"):
        cb0 = combine(1, 0, b0)
    with step("t_ggu0"):
        grad_gate_up(0)
    with step("t_cb1"):
        cb1 = combine(1, 1, b1)
    with step("t_ggu1"):
        grad_gate_up(1)
    with step("t_tko"):
        take_back(0, land_o, out_hbm)
    with step("t_fb0"):
        finish(1, 0, cb0)
    with step("t_fb1"):
        finish(1, 1, cb1)
        land_b = give_back(1)
    with step("t_tkb"):
        take_back(1, land_b, dtok_hbm)
    with step("t_end"):
        for ref, sem in started:
            rdma(ref, ref, sem, (i, e)).wait_send()
        for copy in stores:
            copy.wait()
    assert sems.count == ssem.shape[0], sems.count


def hand_over(*refs):
    n = len(refs) // 2
    sources, targets, sem = refs[:n], refs[n : 2 * n], refs[2 * n]
    copies = []
    for a in range(n):
        lead = sources[a].shape[0]
        cut = 2 if lead > 64 else 1
        for k in range(cut):
            rows = pl.ds(k * (lead // cut), lead // cut)
            copies.append(
                pltpu.make_async_copy(
                    sources[a].at[rows], targets[a].at[rows], sem.at[len(copies)]
                )
            )
    for copy in copies:
        copy.start()
    for copy in copies:
        copy.wait()


def local(shape, tokens, routes, gates, cotangent, w_gate, w_up, w_down):
    nz, ny, nc = shape
    assert nz == ny
    n8 = nz
    tok, features = tokens.shape
    fanout = routes.shape[1]
    xs = 4
    dq, ff = w_gate.shape[1], w_gate.shape[2]
    total = 2 * n8 * nc * n8 * 2
    blk = total // xs
    gt = n8 * tok
    V = pltpu.VMEM
    nsem = 72
    hb = pl.BlockSpec(memory_space=pl.ANY)
    sds = jax.ShapeDtypeStruct
    shapes = (
        sds((tok, features), BF16), sds((tok, features), BF16),
        sds(w_gate.shape, BF16), sds(w_up.shape, BF16), sds(w_down.shape, BF16),
    )
    pin = lambda v: pltpu.with_memory_space_constraint(v, pltpu.HBM)
    results = pl.pallas_call(
        functools.partial(body, (n8, nc, dq, ff, tok)),
        out_shape=shapes,
        in_specs=[pl.BlockSpec(memory_space=pltpu.HBM)] * 7,
        out_specs=(hb,) * 5,
        scratch_shapes=[
            V((fanout, tok), jnp.int32),
            V((fanout, tok), F32),
            V((fanout, 128), jnp.int32),
            V((fanout, 128), F32),
            V((dq, 2 * ff), BF16),
            V((ff, dq), BF16),
            V((xs, fanout, 128), jnp.int32),
            V((xs, fanout, 128), F32),
            V((2, xs, tok, dq), BF16),
            V((2, n8, 2, fanout, 128), jnp.int32),
            V((2, n8, 2, fanout, 128), F32),
            V((2, 2, 2 * gt, dq), BF16),
            V((2, total, 2 * gt), BF16),
            V((2, total, 2 * gt), BF16),
            V((2, total, 2 * gt), BF16),
            V((2, total, 1), F32),
            V((2, 2, total, dq), BF16),
            V((2, 2, total, dq), BF16),
            V((2, total, 2 * ff), BF16),
            V((2, total, ff), BF16),
            V((2, 8, blk, ff), BF16),
            V((2, 8, blk, ff // 2), BF16),
            V((2, total, ff), BF16),
            V((2, total, 2 * ff), BF16),
            V((2, 2, blk, ff), F32),
            V((dq, 2 * ff), F32),
            V((ff, dq), F32),
            V((2, 2, total, dq), BF16),
            V((2, 2, total, dq), BF16),
            V((2, 2, 2 * gt, dq), BF16),
            V((2, 2, 2 * gt, dq), BF16),
            V((2, xs, tok, dq), BF16),
            V((2, xs, tok, dq), BF16),
            V((dq, ff), BF16),
            V((dq, ff), BF16),
            V((ff, dq), BF16),
            V((2, tok, features), BF16),
            pltpu.SemaphoreType.DMA((7,)),
            pltpu.SemaphoreType.DMA((5,)),
            pltpu.SemaphoreType.DMA((nsem,)),
            pltpu.SemaphoreType.DMA((nsem,)),
        ],
        compiler_params=pltpu.CompilerParams(
            collective_id=0, has_side_effects=True, vmem_limit_bytes=48 * 1024 * 1024
        ),
        name="moe_layer",
    )(*map(pin, (routes.T, gates.T, tokens, cotangent, w_gate, w_up, w_down)))
    flat = [r.reshape(-1, r.shape[-1]) for r in results]
    shapes2 = [sds(r.shape, BF16) for r in flat]
    given = pl.pallas_call(
        hand_over,
        out_shape=shapes2,
        in_specs=[hb] * 5,
        out_specs=[hb] * 5,
        scratch_shapes=[pltpu.SemaphoreType.DMA((16,))],
        compiler_params=pltpu.CompilerParams(vmem_limit_bytes=4 * 1024 * 1024),
        name="hand_over",
    )(*flat)
    return tuple(g.reshape(s.shape) for g, s in zip(given, shapes))


def solution(mesh):
    return jax.shard_map(
        functools.partial(local, LAYOUT[mesh.shape["expert"]]),
        mesh=mesh,
        in_specs=(
            P(("dp", "expert"), None),
            P(("dp", "expert"), None),
            P(("dp", "expert"), None),
            P(("dp", "expert"), None),
            P("expert", "dp", None),
            P("expert", "dp", None),
            P("expert", None, "dp"),
        ),
        out_specs=(
            P(("dp", "expert"), None),
            P(("dp", "expert"), None),
            P("expert", "dp", None),
            P("expert", "dp", None),
            P("expert", None, "dp"),
        ),
        check_vma=False,
    )
```

```python
import functools

import jax
import jax.numpy as jnp
from jax import lax
from jax.experimental import pallas as pl
from jax.experimental.pallas import tpu as pltpu
from jax.sharding import PartitionSpec as P

MESH = pl.DeviceIdType.MESH
LAYOUT = {128: (8, 8, 2), 8: (2, 2, 2)}
F32, BF16 = jnp.float32, jnp.bfloat16
CONTRACT_LAST = (((1,), (1,)), ((), ()))
CONTRACT_FIRST = (((0,), (0,)), ((), ()))


def fit(total, want):
    return want if total % want == 0 else total


class Sems:
    def __init__(self):
        self.count = 0

    def take(self, n=1):
        first = self.count
        self.count += n
        return first


def body(
    cfg,
    routes_ref, gates_ref, tok_ref, cot_ref, wg_hbm, wu_hbm, wd_hbm,
    out_hbm, dtok_hbm, gg_hbm, gu_hbm, gd_hbm,
    raw_r, raw_g, own_r, own_g, wgu, wd, xroutes, xgates, xdata, groutes, ggates, gdata,
    dmat, whi, wlo, gcol, rows, recv, pgu, pdh, rgu, rdh, hid, dgu, gate_s, gacc, gdacc,
    ret_s, ret, part, psum, fin, land, gg, gu, gd, tok_out,
    wsem, osem, ssem, rsem,
):
    n8, nc, dq, ff, tok = cfg
    xs = 4
    nq = n8 * nc
    size = 2 * n8
    total = nq * size
    per = nq // xs
    blk = per * size
    gt = n8 * tok
    i = lax.axis_index("dp")
    e = lax.axis_index("expert")
    z, yc = e // nq, e % nq
    y, c = yc // nc, yc % nc
    right, left, opp = (i + 1) % xs, (i + 3) % xs, (i + 2) % xs
    sends, recvs = Sems(), Sems()

    def pick(kind, a, b):
        return jnp.where(kind == 0, a, b)

    me_src = pick(c, z, y)
    me_q = pick(c, yc, z * nc + c)

    def src_dev(p):
        return pick(c, (p * n8 + y) * nc, (z * n8 + p) * nc + 1)

    def q_dev(q):
        return pick(c, z * nq + q, ((q // nc) * n8 + y) * nc + q % nc)

    def block(p):
        return pl.ds(p * size if isinstance(p, int) else pl.multiple_of(p * size, size), size)

    def src_rows(p):
        return pl.ds(pl.multiple_of(p * tok, tok), tok)

    def rdma(src, dst, ss, rs, dev):
        return pltpu.make_async_remote_copy(
            src_ref=src, dst_ref=dst, send_sem=ssem.at[ss], recv_sem=rsem.at[rs],
            device_id=dev, device_id_type=MESH,
        )

    started = []

    def wait_recv(ref, sem):
        rdma(ref, ref, 0, sem, (i, e)).wait_recv()

    def note_send(ref, sem):
        started.append((ref, sem))

    shared = {}

    def send_group(name, view):
        if name not in shared:
            shared[name] = sends.take()
            note_send(view, shared[name])
        return shared[name]

    part_of = lambda ref, k: ref.at[:, pl.ds(pl.multiple_of(k * dq, 128), dq)]
    owns = [
        pltpu.make_async_copy(routes_ref, raw_r, wsem.at[3]),
        pltpu.make_async_copy(part_of(tok_ref, i), xdata.at[0, i], wsem.at[4]),
        pltpu.make_async_copy(gates_ref, raw_g, wsem.at[5]),
        pltpu.make_async_copy(part_of(cot_ref, i), xdata.at[1, i], wsem.at[6]),
    ]
    for own in owns:
        own.start()
    loads = [
        pltpu.make_async_copy(wg_hbm.at[0], wgu.at[:, pl.ds(0, ff)], wsem.at[0]),
        pltpu.make_async_copy(wu_hbm.at[0], wgu.at[:, pl.ds(ff, ff)], wsem.at[1]),
        pltpu.make_async_copy(wd_hbm.at[0], wd, wsem.at[2]),
    ]
    for load in loads:
        load.start()

    with jax.named_scope("h_barrier"):
        barrier = pltpu.get_barrier_semaphore()
        for k in range(1, xs):
            pl.semaphore_signal(barrier, inc=1, device_id=((i + k) % xs, e), device_id_type=MESH)

        @pl.loop(1, nq)
        def _(k):
            peer = z * nq + (yc + k) % nq
            pl.semaphore_signal(barrier, inc=1, device_id=(i, peer), device_id_type=MESH)
            q = (z * nc + c + k) % nq
            peer = ((q // nc) * n8 + y) * nc + q % nc
            pl.semaphore_signal(barrier, inc=1, device_id=(i, peer), device_id_type=MESH)
        for t, raw, tile_ref in ((0, raw_r, own_r), (1, raw_g, own_g)):
            owns[2 * t].wait()
            value = raw[...]
            blank = jnp.zeros((value.shape[0], 128 - tok), value.dtype)
            tile_ref[...] = jnp.concatenate([value, blank], axis=1)
        pl.semaphore_wait(barrier, xs - 1 + 2 * (nq - 1))

    info = ((own_r, xroutes, groutes), (own_g, xgates, ggates))
    data_refs = (tok_ref, cot_ref)
    x_sems = []
    with jax.named_scope("h_x"):
        for t in range(2):
            own, xinfo, _ = info[t]
            x_sems.append((recvs.take(), recvs.take()))
            si, sd = sends.take(), sends.take()
            for k in (2, 1, 3):
                peer = (i + k) % xs
                rdma(own, xinfo.at[i], si, x_sems[t][0], (peer, e)).start()
                rdma(
                    part_of(data_refs[t], peer), xdata.at[t, i], sd, x_sems[t][1], (peer, e)
                ).start()
            xinfo[i] = own[...]
            note_send(xinfo.at[pl.ds(0, xs - 1)], si)
            note_send(xdata.at[t, pl.ds(0, xs - 1)], sd)

    def split_ready(t):
        wait_recv(info[t][1].at[pl.ds(0, xs - 1)], x_sems[t][0])
        wait_recv(xdata.at[t, pl.ds(0, xs - 1)], x_sems[t][1])
        owns[2 * t + 1].wait()

    def gather(t, s):
        got = []
        _, xinfo, ginfo = info[t]
        tiles, feats = pl.ds(0, n8 - 1), pl.ds(0, (n8 - 1) * tok)
        for src, dst, view, ss in (
            (
                xinfo.at[s], ginfo.at[s, me_src], ginfo.at[s, tiles],
                send_group(("info", t), ginfo.at[:, tiles]),
            ),
            (
                xdata.at[t, s], gdata.at[t, s, src_rows(me_src)], gdata.at[t, s, feats],
                send_group(("data", t), gdata.at[t, :, feats]),
            ),
        ):
            rs = recvs.take()

            @pl.loop(1, n8)
            def _(k, src=src, dst=dst, ss=ss, rs=rs):
                rdma(src, dst, ss, rs, (i, src_dev((me_src + k) % n8))).start()
            dst[...] = src[...]
            got.append((view, rs))
        return got

    def wait_all(pairs):
        for view, sem in pairs:
            wait_recv(view, sem)

    others = pl.ds(0, (nq - 1) * size)

    def slots_out(t, s):
        src, dst = rows.at[t, s], recv.at[t, s]
        ss, rs = send_group(("out", t), recv.at[t, :, others]), recvs.take()
        mine = block(2 * pick(c, y, z) + c)

        @pl.loop(1, nq)
        def _(k):
            q = (me_q + k) % nq
            rdma(src.at[block(q)], dst.at[mine], ss, rs, (i, q_dev(q))).start()
        dst[mine] = src[block(me_q)]
        return [(dst.at[others], rs)]

    def slots_back(src, dst, first, count, ss, rs):
        @pl.loop(0, count)
        def _(n):
            p = first + n
            kind, at = p % 2, p // 2
            dev = pick(kind, z * nq + at * nc, (at * n8 + y) * nc + 1)
            there = block(pick(kind, yc, z * nc + c))

            @pl.when(dev != e)
            def _():
                rdma(src.at[block(p)], dst.at[there], ss, rs, (i, dev)).start()

            @pl.when(dev == e)
            def _():
                dst[there] = src[block(p)]

    def tile(ginfo, s):
        return jnp.concatenate([ginfo[s, p][:, :tok] for p in range(n8)], axis=1)

    def matches(s):
        names = tile(groutes, s)
        wanted = q_dev(lax.broadcasted_iota(jnp.int32, (nq, gt), 0))
        return [names[k : k + 1] == wanted for k in range(names.shape[0])]

    before_r = lax.broadcasted_iota(jnp.int32, (gt, gt), 0)
    before_c = lax.broadcasted_iota(jnp.int32, (gt, gt), 1)
    earlier = jnp.where(
        (before_r // tok == before_c // tok) & (before_r < before_c), 1.0, 0.0
    ).astype(BF16)
    slot_r = lax.broadcasted_iota(jnp.int32, (size, gt), 0)
    cell = lax.broadcasted_iota(jnp.int32, (size, gt), 1) // tok == slot_r // 2
    seg0 = jnp.where(cell & (slot_r % 2 == 0), 1.0, 0.0)
    seg1 = jnp.where(cell & (slot_r % 2 == 1), 1.0, 0.0)

    def selection(s):
        hit = jnp.zeros((nq, gt), F32)
        for m in matches(s):
            hit = jnp.where(m, 1.0, hit)
        prior = jnp.dot(hit.astype(BF16), earlier, preferred_element_type=F32)
        first = jnp.where(prior < 0.5, hit, 0.0)
        second = hit - first
        for q in range(nq):
            dmat[s, block(q), :] = (
                seg0 * first[q : q + 1] + seg1 * second[q : q + 1]
            ).astype(BF16)

    def weighting(s):
        values = tile(ggates, s)
        gate = jnp.zeros((nq, gt), F32)
        for k, m in enumerate(matches(s)):
            gate = jnp.where(m, values[k : k + 1], gate)
        for q in range(nq):
            w = dmat[s, block(q), :].astype(F32) * gate[q : q + 1]
            hi = w.astype(BF16)
            whi[s, block(q), :] = hi
            wlo[s, block(q), :] = (w - hi.astype(F32)).astype(BF16)
            gcol[s, block(q), :] = jnp.sum(w, axis=1, keepdims=True)

    def send_rows(t, s):
        picked = jnp.dot(dmat[s], gdata[t, s], preferred_element_type=F32)
        if t == 1:
            picked = picked * gcol[s]
        rows[t, s] = picked.astype(BF16)
        return slots_out(t, s)

    def chunk(k):
        return pl.ds(pl.multiple_of(k * blk, blk), blk)

    def ring_sum_open(name, r):
        return send_group(name, r.at[:, pl.ds(0, 6)]), recvs.take(3)

    def ring_sum_1(p, r, w, sem, slots):
        ss, rs = sem
        a, b = pl.ds(0, w), pl.ds(w, w)
        for slot in slots:
            at, lanes, dev = (
                (opp, a, right), (opp, b, left), (left, a, left), (right, b, right)
            )[slot]
            rdma(
                p.at[chunk(at), lanes], r.at[slot], ss, rs + min(slot, 2), (dev, e)
            ).start()

    def ring_sum_2(p, r, w, sem):
        ss, rs = sem
        for slot, lanes, dev in ((0, pl.ds(0, w), right), (1, pl.ds(w, w), left)):
            wait_recv(r.at[slot], rs + slot)
            r[6 + slot] = (
                r[slot].astype(F32) + p[chunk(dev), lanes].astype(F32)
            ).astype(BF16)
            rdma(r.at[6 + slot], r.at[4 + slot], ss, rs + 2, (dev, e)).start()

    def ring_sum_3(p, r, w, sem):
        wait_recv(r.at[pl.ds(2, 4)], sem[1] + 2)
        a = p[chunk(i), :w].astype(F32) + r[2].astype(F32) + r[4].astype(F32)
        b = p[chunk(i), w:].astype(F32) + r[3].astype(F32) + r[5].astype(F32)
        return a, b

    def ring_gather_open(name, whole):
        return send_group(name, whole.at[:, pl.ds(0, 3 * blk)]), recvs.take(4)

    def ring_gather_1(g, w, sem, half):
        ss, rs = sem
        for k, dev in ((0, right), (1, left)):
            view = g.at[chunk(i), pl.ds((k if half == 0 else 1 - k) * w, w)]
            rdma(view, view, ss, rs + (k if half == 0 else 2), (dev, e)).start()

    def ring_gather_2(g, w, sem):
        ss, rs = sem
        for k, frm, dev in ((0, left, right), (1, right, left)):
            view = g.at[chunk(frm), pl.ds(k * w, w)]
            wait_recv(view, rs + k)
            rdma(view, view, ss, rs + 3, (dev, e)).start()

    def ring_near(g, sem):
        wait_recv(g.at[chunk(left)], sem[1] + 2)

    def ring_gather_3(g, sem):
        wait_recv(g.at[chunk(opp)], sem[1] + 3)

    tf = fit(ff, 256)
    td = fit(dq, 256)

    def gate_up(s):
        ring = ring_sum_open("gu", rgu)
        for k in range(2):
            @pl.loop(0, ff // tf)
            def _(n, k=k):
                cols = pl.ds(pl.multiple_of(k * ff + n * tf, tf), tf)
                pgu[s, :, cols] = jnp.dot(
                    recv[0, s], wgu[:, cols], preferred_element_type=F32
                ).astype(BF16)
            ring_sum_1(pgu.at[s], rgu.at[s], ff, ring, (0, 2) if k == 0 else (1, 3))
        return ring

    def d_hidden(s):
        @pl.loop(0, ff // tf)
        def _(n):
            cols = pl.ds(pl.multiple_of(n * tf, tf), tf)
            pdh[s, :, cols] = lax.dot_general(
                recv[1, s], wd[cols, :], CONTRACT_LAST, preferred_element_type=F32
            ).astype(BF16)
        ring = ring_sum_open("dh", rdh)
        ring_sum_1(pdh.at[s], rdh.at[s], ff // 2, ring, range(4))
        return ring

    def hidden(s, sem):
        gate, up = ring_sum_3(pgu.at[s], rgu.at[s], ff, sem)
        gate_s[s, 0] = gate
        gate_s[s, 1] = up
        hid[s, chunk(i), :] = (gate * jax.nn.sigmoid(gate) * up).astype(BF16)
        ring = ring_gather_open("hid", hid)
        ring_gather_1(hid.at[s], ff // 2, ring, 0)
        ring_gather_1(hid.at[s], ff // 2, ring, 1)
        return ring

    def d_gate_up(s, sem):
        w = ff // 2
        parts = ring_sum_3(pdh.at[s], rdh.at[s], w, sem)
        for k in range(2):
            cols = slice(k * w, (k + 1) * w)
            gate, up, dh = gate_s[s, 0, :, cols], gate_s[s, 1, :, cols], parts[k]
            sig = jax.nn.sigmoid(gate)
            dgu[s, chunk(i), pl.ds(k * w, w)] = (
                dh * up * sig * (1.0 + gate * (1.0 - sig))
            ).astype(BF16)
            dgu[s, chunk(i), pl.ds(ff + k * w, w)] = (dh * (gate * sig)).astype(BF16)
        ring = ring_gather_open("dgu", dgu)
        ring_gather_1(dgu.at[s], ff, ring, 0)
        return ring

    def back_open(t):
        return send_group(("ret", t), ret.at[t, :, others]), recvs.take()

    def all_back(t, s):
        ss, rs = back_open(t)
        slots_back(ret_s.at[t, s], ret.at[t, s], 0, nq, ss, rs)
        return [(ret.at[t, s, others], rs)]

    def out_rows(s):
        @pl.loop(0, dq // td)
        def _(n):
            cols = pl.ds(pl.multiple_of(n * td, td), td)
            ret_s[0, s, :, cols] = jnp.dot(
                hid[s], wd[:, cols], preferred_element_type=F32
            ).astype(BF16)
        return all_back(0, s)

    def back_block(s, at):
        @pl.loop(0, dq // td)
        def _(n):
            cols = pl.ds(pl.multiple_of(n * td, td), td)
            ret_s[1, s, at, cols] = lax.dot_general(
                dgu[s, at], wgu[cols, :], CONTRACT_LAST, preferred_element_type=F32
            ).astype(BF16)

    def back_rows(s):
        back_block(s, slice(None))
        return all_back(1, s)

    def back_send(s, k, sem):
        back_block(s, chunk(k))
        slots_back(ret_s.at[1, s], ret.at[1, s], k * per, per, *sem)

    def combine(t, s, arrived):
        wait_all(arrived)
        got = ret[t, s]
        if t == 0:
            sums = lax.dot_general(
                whi[s], got, CONTRACT_FIRST, preferred_element_type=F32
            ) + lax.dot_general(wlo[s], got, CONTRACT_FIRST, preferred_element_type=F32)
        else:
            sums = lax.dot_general(dmat[s], got, CONTRACT_FIRST, preferred_element_type=F32)
        part[t, s] = sums.astype(BF16)
        feats = pl.ds(0, (n8 - 1) * tok)
        ss, rs = send_group(("sum", t), psum.at[t, :, feats]), recvs.take()
        mine = src_rows(me_src)

        @pl.loop(1, n8)
        def _(k):
            p = (me_src + k) % n8
            rdma(
                part.at[t, s, src_rows(p)], psum.at[t, s, mine], ss, rs, (i, src_dev(p))
            ).start()
        psum[t, s, mine] = part[t, s, mine]
        return [(psum.at[t, s, feats], rs)]

    def finish(t, s, arrived):
        wait_all(arrived)
        acc = psum[t, s, :tok].astype(F32)
        for p in range(1, n8):
            acc = acc + psum[t, s, p * tok : (p + 1) * tok].astype(F32)
        fin[t, s] = acc.astype(BF16)

    def give_back(t):
        ss, rs = sends.take(), recvs.take()
        for k in (2, 1, 3):
            peer = (i + k) % xs
            rdma(fin.at[t, peer], land.at[t, i], ss, rs, (peer, e)).start()
        land[t, i] = fin[t, i]
        view = land.at[t, pl.ds(0, xs - 1)]
        note_send(view, ss)
        return view, rs

    stores = []

    def store(src, dst):
        copy = pltpu.make_async_copy(src, dst, osem.at[len(stores)])
        copy.start()
        stores.append(copy)

    def take_back(t, landed, dst):
        wait_recv(*landed)
        for j in range(xs):
            tok_out[t, :, j * dq : (j + 1) * dq] = land[t, j]
        store(tok_out.at[t], dst)

    def pair(ref, p, cols):
        both = ref[2 * p : 2 * p + 2, :, cols]
        return both.reshape(2 * total, both.shape[-1])

    def grad_down(p):
        @pl.loop(0, ff // tf)
        def _(n):
            cols = pl.ds(pl.multiple_of(n * tf, tf), tf)
            value = lax.dot_general(
                pair(hid, p, cols), pair(recv.at[1], p, slice(None)), CONTRACT_FIRST,
                preferred_element_type=F32,
            )
            if p == 0:
                gdacc[cols, :] = value
            else:
                gd[cols, :] = (gdacc[cols, :] + value).astype(BF16)
        if p == 1:
            store(gd, gd_hbm.at[0])

    def grad_gate_up(p):
        for k, ref, dst in ((0, gg, gg_hbm), (1, gu, gu_hbm)):
            @pl.loop(0, ff // tf)
            def _(n, k=k, ref=ref):
                cols = pl.ds(pl.multiple_of(n * tf, tf), tf)
                both = pl.ds(pl.multiple_of(k * ff + n * tf, tf), tf)
                value = lax.dot_general(
                    pair(recv.at[0], p, slice(None)), pair(dgu, p, both), CONTRACT_FIRST,
                    preferred_element_type=F32,
                )
                if p == 0:
                    gacc[:, both] = value
                else:
                    ref[:, cols] = (gacc[:, both] + value).astype(BF16)
            if p == 1:
                store(ref, dst.at[0])

    step = jax.named_scope
    r, d, u, v, h, g, o, b, co, cb = ([None] * xs for _ in range(10))
    tg, cg = [None] * xs, [None] * xs

    def token_rows(s):
        with step(f"h_sel{s}"):
            wait_recv(*tg[s][0])
            selection(s)
        with step(f"h_rows{s}"):
            wait_recv(*tg[s][1])
            r[s] = send_rows(0, s)

    def cotangent_rows(s):
        with step(f"h_cot{s}"):
            wait_all(cg[s])
            weighting(s)
            d[s] = send_rows(1, s)

    def do_gu(s):
        with step(f"a_wr{s}"):
            wait_all(r[s])
        with step(f"a_gu{s}"):
            u[s] = gate_up(s)

    def do_gu2(s):
        with step(f"a_gur{s}"):
            ring_sum_2(pgu.at[s], rgu.at[s], ff, u[s])

    def do_hid(s):
        with step(f"a_hid{s}"):
            h[s] = hidden(s, u[s])

    def do_hid2(s):
        with step(f"a_hf{s}"):
            ring_gather_2(hid.at[s], ff // 2, h[s])

    def do_dh(s):
        with step(f"a_dh{s}"):
            wait_all(d[s])
            v[s] = d_hidden(s)

    def do_dh2(s):
        with step(f"a_dhr{s}"):
            ring_sum_2(pdh.at[s], rdh.at[s], ff // 2, v[s])

    def do_dg(s):
        with step(f"a_dg{s}"):
            g[s] = d_gate_up(s, v[s])
            if s == 0:
                ring_gather_1(dgu.at[s], ff, g[s], 1)

    def do_dg2(s):
        with step(f"a_dgf{s}"):
            ring_gather_2(dgu.at[s], ff, g[s])
            if s < xs - 1:
                ring_gather_1(dgu.at[s + 1], ff, g[s + 1], 1)

    def do_out(s):
        with step(f"a_wh{s}"):
            ring_near(hid.at[s], h[s])
            ring_gather_3(hid.at[s], h[s])
        with step(f"a_out{s}"):
            o[s] = out_rows(s)

    def do_back(s):
        with step(f"a_wg{s}"):
            ring_near(dgu.at[s], g[s])
            ring_gather_3(dgu.at[s], g[s])
        with step(f"a_back{s}"):
            b[s] = back_rows(s)

    def do_co(s):
        with step(f"a_co{s}"):
            co[s] = combine(0, s, o[s])

    def do_cb(s):
        with step(f"t_cb{s}"):
            cb[s] = combine(1, s, b[s])

    def do_fin(t, s):
        with step(f"t_fin{t}{s}"):
            finish(t, s, (co, cb)[t][s])

    with step("h_wx0"):
        split_ready(0)
        for s in range(3):
            tg[s] = gather(0, s)
    token_rows(0)
    tg[3] = gather(0, 3)
    token_rows(1)
    token_rows(2)
    loads[0].wait()
    loads[1].wait()
    do_gu(0)
    token_rows(3)
    do_gu(1)
    with step("h_gcot"):
        split_ready(1)
        for s in range(xs):
            cg[s] = gather(1, s)
    do_gu2(0)
    do_gu(2)
    cotangent_rows(0)
    do_gu2(1)
    do_hid(0)
    do_gu(3)
    do_gu2(2)
    do_hid(1)
    do_hid2(0)
    cotangent_rows(1)
    loads[2].wait()
    do_dh(0)
    do_gu2(3)
    do_hid(2)
    do_hid2(1)
    cotangent_rows(2)
    do_dh(1)
    do_dh2(0)
    cotangent_rows(3)
    do_out(0)
    do_hid(3)
    do_hid2(2)
    do_dh(2)
    do_dh2(1)
    do_out(1)
    do_dh(3)
    do_hid2(3)
    do_dh2(2)
    do_dg(0)
    do_out(2)
    do_dh2(3)
    do_dg(1)
    do_co(0)
    do_out(3)
    do_dg2(0)
    do_dg(2)
    do_co(1)
    with step("a_gd0"):
        grad_down(0)
    do_dg2(1)
    do_dg(3)
    do_co(2)
    with step("a_gd1"):
        grad_down(1)
    do_fin(0, 0)
    do_back(0)
    do_dg2(2)
    do_co(3)
    do_fin(0, 1)
    do_back(1)
    do_dg2(3)
    do_cb(0)
    do_fin(0, 2)
    do_back(2)
    sem3 = back_open(1)
    with step("t_bk3own"):
        back_send(3, i, sem3)
    do_cb(1)
    with step("t_wnear"):
        ring_near(dgu.at[3], g[3])
    with step("t_bk3lr"):
        back_send(3, left, sem3)
        back_send(3, right, sem3)
    do_fin(0, 3)
    with step("t_wlast"):
        ring_gather_3(dgu.at[3], g[3])
    with step("t_bk3opp"):
        back_send(3, opp, sem3)
        b[3] = [(ret.at[1, 3, others], sem3[1])]
    with step("t_ggu0"):
        grad_gate_up(0)
    do_cb(2)
    with step("t_give0"):
        land_o = give_back(0)
    do_cb(3)
    with step("t_ggu1"):
        grad_gate_up(1)
    with step("t_tko"):
        take_back(0, land_o, out_hbm)
    for s in range(xs):
        do_fin(1, s)
    with step("t_give1"):
        land_b = give_back(1)
    with step("t_tkb"):
        take_back(1, land_b, dtok_hbm)
    with step("t_end"):
        for ref, sem in started:
            rdma(ref, ref, sem, 0, (i, e)).wait_send()
        for copy in stores:
            copy.wait()
    assert (sends.count, recvs.count) == (ssem.shape[0], rsem.shape[0]), (
        sends.count, recvs.count
    )


def hand_over(*refs):
    n = len(refs) // 2
    sources, targets, sem = refs[:n], refs[n : 2 * n], refs[2 * n]
    copies = []
    for a in range(n):
        lead = sources[a].shape[0]
        cut = 2 if lead > 64 else 1
        for k in range(cut):
            rows = pl.ds(k * (lead // cut), lead // cut)
            copies.append(
                pltpu.make_async_copy(
                    sources[a].at[rows], targets[a].at[rows], sem.at[len(copies)]
                )
            )
    for copy in copies:
        copy.start()
    for copy in copies:
        copy.wait()


def local(shape, tokens, routes, gates, cotangent, w_gate, w_up, w_down):
    nz, ny, nc = shape
    assert nz == ny
    n8 = nz
    tok, features = tokens.shape
    fanout = routes.shape[1]
    xs = 4
    dq, ff = w_gate.shape[1], w_gate.shape[2]
    total = n8 * nc * n8 * 2
    blk = total // xs
    gt = n8 * tok
    V = pltpu.VMEM
    hb = pl.BlockSpec(memory_space=pl.ANY)
    sds = jax.ShapeDtypeStruct
    shapes = (
        sds((tok, features), BF16), sds((tok, features), BF16),
        sds(w_gate.shape, BF16), sds(w_up.shape, BF16), sds(w_down.shape, BF16),
    )
    pin = lambda v: pltpu.with_memory_space_constraint(v, pltpu.HBM)
    results = pl.pallas_call(
        functools.partial(body, (n8, nc, dq, ff, tok)),
        out_shape=shapes,
        in_specs=[pl.BlockSpec(memory_space=pltpu.HBM)] * 7,
        out_specs=(hb,) * 5,
        scratch_shapes=[
            V((fanout, tok), jnp.int32),
            V((fanout, tok), F32),
            V((fanout, 128), jnp.int32),
            V((fanout, 128), F32),
            V((dq, 2 * ff), BF16),
            V((ff, dq), BF16),
            V((xs, fanout, 128), jnp.int32),
            V((xs, fanout, 128), F32),
            V((2, xs, tok, dq), BF16),
            V((xs, n8, fanout, 128), jnp.int32),
            V((xs, n8, fanout, 128), F32),
            V((2, xs, gt, dq), BF16),
            V((xs, total, gt), BF16),
            V((xs, total, gt), BF16),
            V((xs, total, gt), BF16),
            V((xs, total, 1), F32),
            V((2, xs, total, dq), BF16),
            V((2, xs, total, dq), BF16),
            V((xs, total, 2 * ff), BF16),
            V((xs, total, ff), BF16),
            V((xs, 8, blk, ff), BF16),
            V((xs, 8, blk, ff // 2), BF16),
            V((xs, total, ff), BF16),
            V((xs, total, 2 * ff), BF16),
            V((xs, 2, blk, ff), F32),
            V((dq, 2 * ff), F32),
            V((ff, dq), F32),
            V((2, xs, total, dq), BF16),
            V((2, xs, total, dq), BF16),
            V((2, xs, gt, dq), BF16),
            V((2, xs, gt, dq), BF16),
            V((2, xs, tok, dq), BF16),
            V((2, xs, tok, dq), BF16),
            V((dq, ff), BF16),
            V((dq, ff), BF16),
            V((ff, dq), BF16),
            V((2, tok, features), BF16),
            pltpu.SemaphoreType.DMA((7,)),
            pltpu.SemaphoreType.DMA((5,)),
            pltpu.SemaphoreType.DMA((20,)),
            pltpu.SemaphoreType.DMA((102,)),
        ],
        compiler_params=pltpu.CompilerParams(
            collective_id=0, has_side_effects=True, vmem_limit_bytes=48 * 1024 * 1024
        ),
        name="moe_layer",
    )(*map(pin, (routes.T, gates.T, tokens, cotangent, w_gate, w_up, w_down)))
    flat = [r.reshape(-1, r.shape[-1]) for r in results]
    shapes2 = [sds(r.shape, BF16) for r in flat]
    given = pl.pallas_call(
        hand_over,
        out_shape=shapes2,
        in_specs=[hb] * 5,
        out_specs=[hb] * 5,
        scratch_shapes=[pltpu.SemaphoreType.DMA((16,))],
        compiler_params=pltpu.CompilerParams(vmem_limit_bytes=4 * 1024 * 1024),
        name="hand_over",
    )(*flat)
    return tuple(g.reshape(s.shape) for g, s in zip(given, shapes))


def solution(mesh):
    return jax.shard_map(
        functools.partial(local, LAYOUT[mesh.shape["expert"]]),
        mesh=mesh,
        in_specs=(
            P(("dp", "expert"), None),
            P(("dp", "expert"), None),
            P(("dp", "expert"), None),
            P(("dp", "expert"), None),
            P("expert", "dp", None),
            P("expert", "dp", None),
            P("expert", None, "dp"),
        ),
        out_specs=(
            P(("dp", "expert"), None),
            P(("dp", "expert"), None),
            P("expert", "dp", None),
            P("expert", "dp", None),
            P("expert", None, "dp"),
        ),
        check_vma=False,
    )
```

```python
import functools

import jax
import jax.numpy as jnp
from jax import lax
from jax.experimental import pallas as pl
from jax.experimental.pallas import tpu as pltpu
from jax.sharding import PartitionSpec as P

MESH = pl.DeviceIdType.MESH
LAYOUT = {128: (8, 8, 2), 8: (2, 2, 2)}
F32, BF16 = jnp.float32, jnp.bfloat16
CONTRACT_LAST = (((1,), (1,)), ((), ()))
CONTRACT_FIRST = (((0,), (0,)), ((), ()))


def fit(total, want):
    return want if total % want == 0 else total


class Sems:
    def __init__(self):
        self.count = 0

    def take(self, n=1):
        first = self.count
        self.count += n
        return first


def body(
    cfg,
    routes_ref, gates_ref, tok_ref, cot_ref, wg_hbm, wu_hbm, wd_hbm,
    out_hbm, dtok_hbm, gg_hbm, gu_hbm, gd_hbm,
    raw_r, raw_g, own_r, own_g, wgu, wd, xroutes, xgates, xdata, groutes, ggates, gdata,
    dmat, whi, wlo, gcol, rows, recv, pgu, pdh, rgu, rdh, hid, dgu, gate_s, gacc, gdacc,
    ret_s, ret, part, psum, fin, land, gg, gu, gd, tok_out,
    wsem, osem, ssem, rsem,
):
    n8, nc, dq, ff, tok = cfg
    xs = 4
    nq = n8 * nc
    size = 2 * n8
    total = nq * size
    per = nq // xs
    blk = per * size
    gt = n8 * tok
    i = lax.axis_index("dp")
    e = lax.axis_index("expert")
    z, yc = e // nq, e % nq
    y, c = yc // nc, yc % nc
    right, left, opp = (i + 1) % xs, (i + 3) % xs, (i + 2) % xs
    sends, recvs = Sems(), Sems()

    def pick(kind, a, b):
        return jnp.where(kind == 0, a, b)

    me_src = pick(c, z, y)
    me_q = pick(c, yc, z * nc + c)

    def src_dev(p):
        return pick(c, (p * n8 + y) * nc, (z * n8 + p) * nc + 1)

    def q_dev(q):
        return pick(c, z * nq + q, ((q // nc) * n8 + y) * nc + q % nc)

    def block(p):
        return pl.ds(p * size if isinstance(p, int) else pl.multiple_of(p * size, size), size)

    def src_rows(p):
        return pl.ds(pl.multiple_of(p * tok, tok), tok)

    def rdma(src, dst, ss, rs, dev):
        return pltpu.make_async_remote_copy(
            src_ref=src, dst_ref=dst, send_sem=ssem.at[ss], recv_sem=rsem.at[rs],
            device_id=dev, device_id_type=MESH,
        )

    started = []

    def wait_recv(ref, sem):
        rdma(ref, ref, 0, sem, (i, e)).wait_recv()

    def note_send(ref, sem):
        started.append((ref, sem))

    shared = {}

    def send_group(name, view):
        if name not in shared:
            shared[name] = sends.take()
            note_send(view, shared[name])
        return shared[name]

    part_of = lambda ref, k: ref.at[:, pl.ds(pl.multiple_of(k * dq, 128), dq)]
    owns = [
        pltpu.make_async_copy(routes_ref, raw_r, wsem.at[3]),
        pltpu.make_async_copy(part_of(tok_ref, i), xdata.at[0, i], wsem.at[4]),
        pltpu.make_async_copy(gates_ref, raw_g, wsem.at[5]),
        pltpu.make_async_copy(part_of(cot_ref, i), xdata.at[1, i], wsem.at[6]),
    ]
    loads = [
        pltpu.make_async_copy(wg_hbm.at[0], wgu.at[:, pl.ds(0, ff)], wsem.at[0]),
        pltpu.make_async_copy(wu_hbm.at[0], wgu.at[:, pl.ds(ff, ff)], wsem.at[1]),
        pltpu.make_async_copy(wd_hbm.at[0], wd, wsem.at[2]),
    ]

    with jax.named_scope("h_barrier"):
        barrier = pltpu.get_barrier_semaphore()
        for k in range(1, xs):
            pl.semaphore_signal(barrier, inc=1, device_id=((i + k) % xs, e), device_id_type=MESH)

        @pl.loop(1, nq)
        def _(k):
            peer = z * nq + (yc + k) % nq
            pl.semaphore_signal(barrier, inc=1, device_id=(i, peer), device_id_type=MESH)
            q = (z * nc + c + k) % nq
            peer = ((q // nc) * n8 + y) * nc + q % nc
            pl.semaphore_signal(barrier, inc=1, device_id=(i, peer), device_id_type=MESH)
        for copy in owns + loads:
            copy.start()
        pl.semaphore_wait(barrier, xs - 1 + 2 * (nq - 1))

    info = ((own_r, xroutes, groutes), (own_g, xgates, ggates))
    data_refs = (tok_ref, cot_ref)
    x_sems = []
    with jax.named_scope("h_x"):
        for t in range(2):
            own, xinfo, _ = info[t]
            x_sems.append((recvs.take(), recvs.take()))
            si, sd = sends.take(), sends.take()
            for k in (2, 1, 3):
                peer = (i + k) % xs
                rdma(
                    part_of(data_refs[t], peer), xdata.at[t, i], sd, x_sems[t][1], (peer, e)
                ).start()
            raw = (raw_r, raw_g)[t]
            owns[2 * t].wait()
            value = raw[...]
            blank = jnp.zeros((value.shape[0], 128 - tok), value.dtype)
            own[...] = jnp.concatenate([value, blank], axis=1)
            xinfo[i] = own[...]
            for k in (2, 1, 3):
                rdma(own, xinfo.at[i], si, x_sems[t][0], ((i + k) % xs, e)).start()
            note_send(xinfo.at[pl.ds(0, xs - 1)], si)
            note_send(xdata.at[t, pl.ds(0, xs - 1)], sd)

    def split_ready(t):
        wait_recv(info[t][1].at[pl.ds(0, xs - 1)], x_sems[t][0])
        wait_recv(xdata.at[t, pl.ds(0, xs - 1)], x_sems[t][1])
        owns[2 * t + 1].wait()

    def gather(t, s):
        got = []
        _, xinfo, ginfo = info[t]
        tiles, feats = pl.ds(0, n8 - 1), pl.ds(0, (n8 - 1) * tok)
        for src, dst, view, ss in (
            (
                xinfo.at[s], ginfo.at[s, me_src], ginfo.at[s, tiles],
                send_group(("info", t), ginfo.at[:, tiles]),
            ),
            (
                xdata.at[t, s], gdata.at[t, s, src_rows(me_src)], gdata.at[t, s, feats],
                send_group(("data", t), gdata.at[t, :, feats]),
            ),
        ):
            rs = recvs.take()

            @pl.loop(1, n8)
            def _(k, src=src, dst=dst, ss=ss, rs=rs):
                rdma(src, dst, ss, rs, (i, src_dev((me_src + k) % n8))).start()
            dst[...] = src[...]
            got.append((view, rs))
        return got

    def wait_all(pairs):
        for view, sem in pairs:
            wait_recv(view, sem)

    others = pl.ds(0, (nq - 1) * size)

    def slots_out(t, s):
        src, dst = rows.at[t, s], recv.at[t, s]
        ss, rs = send_group(("out", t), recv.at[t, :, others]), recvs.take()
        mine = block(2 * pick(c, y, z) + c)

        @pl.loop(1, nq)
        def _(k):
            q = (me_q + k) % nq
            rdma(src.at[block(q)], dst.at[mine], ss, rs, (i, q_dev(q))).start()
        dst[mine] = src[block(me_q)]
        return [(dst.at[others], rs)]

    def slots_back(src, dst, first, count, ss, rs):
        @pl.loop(0, count)
        def _(n):
            p = first + n
            kind, at = p % 2, p // 2
            dev = pick(kind, z * nq + at * nc, (at * n8 + y) * nc + 1)
            there = block(pick(kind, yc, z * nc + c))

            @pl.when(dev != e)
            def _():
                rdma(src.at[block(p)], dst.at[there], ss, rs, (i, dev)).start()

            @pl.when(dev == e)
            def _():
                dst[there] = src[block(p)]

    def tile(ginfo, s):
        return jnp.concatenate([ginfo[s, p][:, :tok] for p in range(n8)], axis=1)

    def matches(s):
        names = tile(groutes, s)
        wanted = q_dev(lax.broadcasted_iota(jnp.int32, (nq, gt), 0))
        return [names[k : k + 1] == wanted for k in range(names.shape[0])]

    before_r = lax.broadcasted_iota(jnp.int32, (gt, gt), 0)
    before_c = lax.broadcasted_iota(jnp.int32, (gt, gt), 1)
    earlier = jnp.where(
        (before_r // tok == before_c // tok) & (before_r < before_c), 1.0, 0.0
    ).astype(BF16)
    slot_r = lax.broadcasted_iota(jnp.int32, (size, gt), 0)
    cell = lax.broadcasted_iota(jnp.int32, (size, gt), 1) // tok == slot_r // 2
    seg0 = jnp.where(cell & (slot_r % 2 == 0), 1.0, 0.0)
    seg1 = jnp.where(cell & (slot_r % 2 == 1), 1.0, 0.0)

    def selection(s):
        hit = jnp.zeros((nq, gt), F32)
        for m in matches(s):
            hit = jnp.where(m, 1.0, hit)
        prior = jnp.dot(hit.astype(BF16), earlier, preferred_element_type=F32)
        first = jnp.where(prior < 0.5, hit, 0.0)
        second = hit - first
        for q in range(nq):
            dmat[s, block(q), :] = (
                seg0 * first[q : q + 1] + seg1 * second[q : q + 1]
            ).astype(BF16)

    def weighting(s):
        values = tile(ggates, s)
        gate = jnp.zeros((nq, gt), F32)
        for k, m in enumerate(matches(s)):
            gate = jnp.where(m, values[k : k + 1], gate)
        for q in range(nq):
            w = dmat[s, block(q), :].astype(F32) * gate[q : q + 1]
            hi = w.astype(BF16)
            whi[s, block(q), :] = hi
            wlo[s, block(q), :] = (w - hi.astype(F32)).astype(BF16)
            gcol[s, block(q), :] = jnp.sum(w, axis=1, keepdims=True)

    def send_rows(t, s):
        picked = jnp.dot(dmat[s], gdata[t, s], preferred_element_type=F32)
        if t == 1:
            picked = picked * gcol[s]
        rows[t, s] = picked.astype(BF16)
        return slots_out(t, s)

    def chunk(k):
        return pl.ds(pl.multiple_of(k * blk, blk), blk)

    def ring_sum_open(name, r):
        return send_group(name, r.at[:, pl.ds(0, 6)]), recvs.take(3)

    def ring_sum_1(p, r, w, sem, slots):
        ss, rs = sem
        a, b = pl.ds(0, w), pl.ds(w, w)
        for slot in slots:
            at, lanes, dev = (
                (opp, a, right), (opp, b, left), (left, a, left), (right, b, right)
            )[slot]
            rdma(
                p.at[chunk(at), lanes], r.at[slot], ss, rs + min(slot, 2), (dev, e)
            ).start()

    def ring_sum_2(p, r, w, sem):
        ss, rs = sem
        for slot, lanes, dev in ((0, pl.ds(0, w), right), (1, pl.ds(w, w), left)):
            wait_recv(r.at[slot], rs + slot)
            r[6 + slot] = (
                r[slot].astype(F32) + p[chunk(dev), lanes].astype(F32)
            ).astype(BF16)
            rdma(r.at[6 + slot], r.at[4 + slot], ss, rs + 2, (dev, e)).start()

    def ring_sum_3(p, r, w, sem):
        wait_recv(r.at[pl.ds(2, 4)], sem[1] + 2)
        a = p[chunk(i), :w].astype(F32) + r[2].astype(F32) + r[4].astype(F32)
        b = p[chunk(i), w:].astype(F32) + r[3].astype(F32) + r[5].astype(F32)
        return a, b

    def ring_gather_open(name, whole):
        return send_group(name, whole.at[:, pl.ds(0, 3 * blk)]), recvs.take(4)

    def ring_gather_1(g, w, sem, half):
        ss, rs = sem
        for k, dev in ((0, right), (1, left)):
            view = g.at[chunk(i), pl.ds((k if half == 0 else 1 - k) * w, w)]
            rdma(view, view, ss, rs + (k if half == 0 else 2), (dev, e)).start()

    def ring_gather_2(g, w, sem):
        ss, rs = sem
        for k, frm, dev in ((0, left, right), (1, right, left)):
            view = g.at[chunk(frm), pl.ds(k * w, w)]
            wait_recv(view, rs + k)
            rdma(view, view, ss, rs + 3, (dev, e)).start()

    def ring_near(g, sem):
        wait_recv(g.at[chunk(left)], sem[1] + 2)

    def ring_gather_3(g, sem):
        wait_recv(g.at[chunk(opp)], sem[1] + 3)

    tf = fit(ff, 256)
    td = fit(dq, 256)

    def gate_up(s):
        ring = ring_sum_open("gu", rgu)
        for k in range(2):
            @pl.loop(0, ff // tf)
            def _(n, k=k):
                cols = pl.ds(pl.multiple_of(k * ff + n * tf, tf), tf)
                pgu[s, :, cols] = jnp.dot(
                    recv[0, s], wgu[:, cols], preferred_element_type=F32
                ).astype(BF16)
            ring_sum_1(pgu.at[s], rgu.at[s], ff, ring, (0, 2) if k == 0 else (1, 3))
        return ring

    def d_hidden(s):
        @pl.loop(0, ff // tf)
        def _(n):
            cols = pl.ds(pl.multiple_of(n * tf, tf), tf)
            pdh[s, :, cols] = lax.dot_general(
                recv[1, s], wd[cols, :], CONTRACT_LAST, preferred_element_type=F32
            ).astype(BF16)
        ring = ring_sum_open("dh", rdh)
        ring_sum_1(pdh.at[s], rdh.at[s], ff // 2, ring, range(4))
        return ring

    def hidden(s, sem):
        gate, up = ring_sum_3(pgu.at[s], rgu.at[s], ff, sem)
        gate_s[s, 0] = gate
        gate_s[s, 1] = up
        hid[s, chunk(i), :] = (gate * jax.nn.sigmoid(gate) * up).astype(BF16)
        ring = ring_gather_open("hid", hid)
        ring_gather_1(hid.at[s], ff // 2, ring, 0)
        ring_gather_1(hid.at[s], ff // 2, ring, 1)
        return ring

    def d_gate_up(s, sem):
        w = ff // 2
        parts = ring_sum_3(pdh.at[s], rdh.at[s], w, sem)
        for k in range(2):
            cols = slice(k * w, (k + 1) * w)
            gate, up, dh = gate_s[s, 0, :, cols], gate_s[s, 1, :, cols], parts[k]
            sig = jax.nn.sigmoid(gate)
            dgu[s, chunk(i), pl.ds(k * w, w)] = (
                dh * up * sig * (1.0 + gate * (1.0 - sig))
            ).astype(BF16)
            dgu[s, chunk(i), pl.ds(ff + k * w, w)] = (dh * (gate * sig)).astype(BF16)
        ring = ring_gather_open("dgu", dgu)
        ring_gather_1(dgu.at[s], ff, ring, 0)
        return ring

    def back_open(t):
        return send_group(("ret", t), ret.at[t, :, others]), recvs.take()

    def all_back(t, s):
        ss, rs = back_open(t)
        slots_back(ret_s.at[t, s], ret.at[t, s], 0, nq, ss, rs)
        return [(ret.at[t, s, others], rs)]

    def out_rows(s):
        @pl.loop(0, dq // td)
        def _(n):
            cols = pl.ds(pl.multiple_of(n * td, td), td)
            ret_s[0, s, :, cols] = jnp.dot(
                hid[s], wd[:, cols], preferred_element_type=F32
            ).astype(BF16)
        return all_back(0, s)

    def back_block(s, at):
        @pl.loop(0, dq // td)
        def _(n):
            cols = pl.ds(pl.multiple_of(n * td, td), td)
            ret_s[1, s, at, cols] = lax.dot_general(
                dgu[s, at], wgu[cols, :], CONTRACT_LAST, preferred_element_type=F32
            ).astype(BF16)

    def back_rows(s):
        back_block(s, slice(None))
        return all_back(1, s)

    def back_send(s, k, sem):
        back_block(s, chunk(k))
        slots_back(ret_s.at[1, s], ret.at[1, s], k * per, per, *sem)

    def combine(t, s, arrived):
        wait_all(arrived)
        got = ret[t, s]
        if t == 0:
            sums = lax.dot_general(
                whi[s], got, CONTRACT_FIRST, preferred_element_type=F32
            ) + lax.dot_general(wlo[s], got, CONTRACT_FIRST, preferred_element_type=F32)
        else:
            sums = lax.dot_general(dmat[s], got, CONTRACT_FIRST, preferred_element_type=F32)
        part[t, s] = sums.astype(BF16)
        feats = pl.ds(0, (n8 - 1) * tok)
        ss, rs = send_group(("sum", t), psum.at[t, :, feats]), recvs.take()
        mine = src_rows(me_src)

        @pl.loop(1, n8)
        def _(k):
            p = (me_src + k) % n8
            rdma(
                part.at[t, s, src_rows(p)], psum.at[t, s, mine], ss, rs, (i, src_dev(p))
            ).start()
        psum[t, s, mine] = part[t, s, mine]
        return [(psum.at[t, s, feats], rs)]

    def finish(t, s, arrived):
        wait_all(arrived)
        acc = psum[t, s, :tok].astype(F32)
        for p in range(1, n8):
            acc = acc + psum[t, s, p * tok : (p + 1) * tok].astype(F32)
        fin[t, s] = acc.astype(BF16)

    def give_back(t):
        ss, rs = sends.take(), recvs.take()
        for k in (2, 1, 3):
            peer = (i + k) % xs
            rdma(fin.at[t, peer], land.at[t, i], ss, rs, (peer, e)).start()
        land[t, i] = fin[t, i]
        view = land.at[t, pl.ds(0, xs - 1)]
        note_send(view, ss)
        return view, rs

    stores = []

    def store(src, dst):
        copy = pltpu.make_async_copy(src, dst, osem.at[len(stores)])
        copy.start()
        stores.append(copy)

    def take_back(t, landed, dst):
        wait_recv(*landed)
        for j in range(xs):
            tok_out[t, :, j * dq : (j + 1) * dq] = land[t, j]
        store(tok_out.at[t], dst)

    def pair(ref, p, cols):
        both = ref[2 * p : 2 * p + 2, :, cols]
        return both.reshape(2 * total, both.shape[-1])

    def grad_down(p):
        @pl.loop(0, ff // tf)
        def _(n):
            cols = pl.ds(pl.multiple_of(n * tf, tf), tf)
            value = lax.dot_general(
                pair(hid, p, cols), pair(recv.at[1], p, slice(None)), CONTRACT_FIRST,
                preferred_element_type=F32,
            )
            if p == 0:
                gdacc[cols, :] = value
            else:
                gd[cols, :] = (gdacc[cols, :] + value).astype(BF16)
        if p == 1:
            store(gd, gd_hbm.at[0])

    def grad_gate_up(p):
        for k, ref, dst in ((0, gg, gg_hbm), (1, gu, gu_hbm)):
            @pl.loop(0, ff // tf)
            def _(n, k=k, ref=ref):
                cols = pl.ds(pl.multiple_of(n * tf, tf), tf)
                both = pl.ds(pl.multiple_of(k * ff + n * tf, tf), tf)
                value = lax.dot_general(
                    pair(recv.at[0], p, slice(None)), pair(dgu, p, both), CONTRACT_FIRST,
                    preferred_element_type=F32,
                )
                if p == 0:
                    gacc[:, both] = value
                else:
                    ref[:, cols] = (gacc[:, both] + value).astype(BF16)
            if p == 1:
                store(ref, dst.at[0])

    step = jax.named_scope
    r, d, u, v, h, g, o, b, co, cb = ([None] * xs for _ in range(10))
    tg, cg = [None] * xs, [None] * xs

    def token_rows(s):
        with step(f"h_sel{s}"):
            wait_recv(*tg[s][0])
            selection(s)
        with step(f"h_rows{s}"):
            wait_recv(*tg[s][1])
            r[s] = send_rows(0, s)

    def cotangent_rows(s):
        with step(f"h_cot{s}"):
            wait_all(cg[s])
            weighting(s)
            d[s] = send_rows(1, s)

    def do_gu(s):
        with step(f"a_wr{s}"):
            wait_all(r[s])
        with step(f"a_gu{s}"):
            u[s] = gate_up(s)

    def do_gu2(s):
        with step(f"a_gur{s}"):
            ring_sum_2(pgu.at[s], rgu.at[s], ff, u[s])

    def do_hid(s):
        with step(f"a_hid{s}"):
            h[s] = hidden(s, u[s])

    def do_hid2(s):
        with step(f"a_hf{s}"):
            ring_gather_2(hid.at[s], ff // 2, h[s])

    def do_dh(s):
        with step(f"a_dh{s}"):
            wait_all(d[s])
            v[s] = d_hidden(s)

    def do_dh2(s):
        with step(f"a_dhr{s}"):
            ring_sum_2(pdh.at[s], rdh.at[s], ff // 2, v[s])

    def do_dg(s):
        with step(f"a_dg{s}"):
            g[s] = d_gate_up(s, v[s])
            if s == 0:
                ring_gather_1(dgu.at[s], ff, g[s], 1)

    def do_dg2(s):
        with step(f"a_dgf{s}"):
            ring_gather_2(dgu.at[s], ff, g[s])
            if s < xs - 1:
                ring_gather_1(dgu.at[s + 1], ff, g[s + 1], 1)

    def do_out(s):
        with step(f"a_wh{s}"):
            ring_near(hid.at[s], h[s])
            ring_gather_3(hid.at[s], h[s])
        with step(f"a_out{s}"):
            o[s] = out_rows(s)

    def do_back(s):
        with step(f"a_wg{s}"):
            ring_near(dgu.at[s], g[s])
            ring_gather_3(dgu.at[s], g[s])
        with step(f"a_back{s}"):
            b[s] = back_rows(s)

    def do_co(s):
        with step(f"a_co{s}"):
            co[s] = combine(0, s, o[s])

    def do_cb(s):
        with step(f"t_cb{s}"):
            cb[s] = combine(1, s, b[s])

    def do_fin(t, s):
        with step(f"t_fin{t}{s}"):
            finish(t, s, (co, cb)[t][s])

    with step("h_wx0"):
        split_ready(0)
        for s in range(3):
            tg[s] = gather(0, s)
    token_rows(0)
    tg[3] = gather(0, 3)
    token_rows(1)
    token_rows(2)
    loads[0].wait()
    loads[1].wait()
    do_gu(0)
    token_rows(3)
    do_gu(1)
    with step("h_gcot"):
        split_ready(1)
        for s in range(xs):
            cg[s] = gather(1, s)
    do_gu2(0)
    do_gu(2)
    cotangent_rows(0)
    do_gu2(1)
    do_hid(0)
    do_gu(3)
    do_gu2(2)
    do_hid(1)
    do_hid2(0)
    cotangent_rows(1)
    loads[2].wait()
    do_dh(0)
    do_gu2(3)
    do_hid(2)
    do_hid2(1)
    cotangent_rows(2)
    do_dh(1)
    do_dh2(0)
    cotangent_rows(3)
    do_out(0)
    do_hid(3)
    do_hid2(2)
    do_dh(2)
    do_dh2(1)
    do_out(1)
    do_dh(3)
    do_hid2(3)
    do_dh2(2)
    do_dg(0)
    do_out(2)
    do_dh2(3)
    do_dg(1)
    do_co(0)
    do_out(3)
    do_dg2(0)
    do_dg(2)
    do_co(1)
    with step("a_gd0"):
        grad_down(0)
    do_dg2(1)
    do_dg(3)
    do_co(2)
    with step("a_gd1"):
        grad_down(1)
    do_fin(0, 0)
    do_back(0)
    do_dg2(2)
    do_co(3)
    do_fin(0, 1)
    do_back(1)
    do_dg2(3)
    do_cb(0)
    do_fin(0, 2)
    do_back(2)
    sem3 = back_open(1)
    with step("t_bk3own"):
        back_send(3, i, sem3)
    with step("t_wnear"):
        ring_near(dgu.at[3], g[3])
    with step("t_bk3lr"):
        back_send(3, left, sem3)
        back_send(3, right, sem3)
    do_fin(0, 3)
    with step("t_wlast"):
        ring_gather_3(dgu.at[3], g[3])
    with step("t_bk3opp"):
        back_send(3, opp, sem3)
        b[3] = [(ret.at[1, 3, others], sem3[1])]
    do_cb(1)
    with step("t_ggu0"):
        grad_gate_up(0)
    do_cb(2)
    with step("t_give0"):
        land_o = give_back(0)
    do_cb(3)
    with step("t_ggu1"):
        grad_gate_up(1)
    with step("t_tko"):
        take_back(0, land_o, out_hbm)
    for s in range(xs):
        do_fin(1, s)
    with step("t_give1"):
        land_b = give_back(1)
    with step("t_tkb"):
        take_back(1, land_b, dtok_hbm)
    with step("t_end"):
        for ref, sem in started:
            rdma(ref, ref, sem, 0, (i, e)).wait_send()
        for copy in stores:
            copy.wait()
    assert (sends.count, recvs.count) == (ssem.shape[0], rsem.shape[0]), (
        sends.count, recvs.count
    )


def hand_over(*refs):
    n = len(refs) // 2
    sources, targets, sem = refs[:n], refs[n : 2 * n], refs[2 * n]
    copies = []
    for a in range(n):
        lead = sources[a].shape[0]
        cut = 2 if lead > 64 else 1
        for k in range(cut):
            rows = pl.ds(k * (lead // cut), lead // cut)
            copies.append(
                pltpu.make_async_copy(
                    sources[a].at[rows], targets[a].at[rows], sem.at[len(copies)]
                )
            )
    for copy in copies:
        copy.start()
    for copy in copies:
        copy.wait()


def local(shape, tokens, routes, gates, cotangent, w_gate, w_up, w_down):
    nz, ny, nc = shape
    assert nz == ny
    n8 = nz
    tok, features = tokens.shape
    fanout = routes.shape[1]
    xs = 4
    dq, ff = w_gate.shape[1], w_gate.shape[2]
    total = n8 * nc * n8 * 2
    blk = total // xs
    gt = n8 * tok
    V = pltpu.VMEM
    hb = pl.BlockSpec(memory_space=pl.ANY)
    sds = jax.ShapeDtypeStruct
    shapes = (
        sds((tok, features), BF16), sds((tok, features), BF16),
        sds(w_gate.shape, BF16), sds(w_up.shape, BF16), sds(w_down.shape, BF16),
    )
    pin = lambda v: pltpu.with_memory_space_constraint(v, pltpu.HBM)
    results = pl.pallas_call(
        functools.partial(body, (n8, nc, dq, ff, tok)),
        out_shape=shapes,
        in_specs=[pl.BlockSpec(memory_space=pltpu.HBM)] * 7,
        out_specs=(hb,) * 5,
        scratch_shapes=[
            V((fanout, tok), jnp.int32),
            V((fanout, tok), F32),
            V((fanout, 128), jnp.int32),
            V((fanout, 128), F32),
            V((dq, 2 * ff), BF16),
            V((ff, dq), BF16),
            V((xs, fanout, 128), jnp.int32),
            V((xs, fanout, 128), F32),
            V((2, xs, tok, dq), BF16),
            V((xs, n8, fanout, 128), jnp.int32),
            V((xs, n8, fanout, 128), F32),
            V((2, xs, gt, dq), BF16),
            V((xs, total, gt), BF16),
            V((xs, total, gt), BF16),
            V((xs, total, gt), BF16),
            V((xs, total, 1), F32),
            V((2, xs, total, dq), BF16),
            V((2, xs, total, dq), BF16),
            V((xs, total, 2 * ff), BF16),
            V((xs, total, ff), BF16),
            V((xs, 8, blk, ff), BF16),
            V((xs, 8, blk, ff // 2), BF16),
            V((xs, total, ff), BF16),
            V((xs, total, 2 * ff), BF16),
            V((xs, 2, blk, ff), F32),
            V((dq, 2 * ff), F32),
            V((ff, dq), F32),
            V((2, xs, total, dq), BF16),
            V((2, xs, total, dq), BF16),
            V((2, xs, gt, dq), BF16),
            V((2, xs, gt, dq), BF16),
            V((2, xs, tok, dq), BF16),
            V((2, xs, tok, dq), BF16),
            V((dq, ff), BF16),
            V((dq, ff), BF16),
            V((ff, dq), BF16),
            V((2, tok, features), BF16),
            pltpu.SemaphoreType.DMA((7,)),
            pltpu.SemaphoreType.DMA((5,)),
            pltpu.SemaphoreType.DMA((20,)),
            pltpu.SemaphoreType.DMA((102,)),
        ],
        compiler_params=pltpu.CompilerParams(
            collective_id=0, has_side_effects=True, vmem_limit_bytes=48 * 1024 * 1024
        ),
        name="moe_layer",
    )(*map(pin, (routes.T, gates.T, tokens, cotangent, w_gate, w_up, w_down)))
    flat = [r.reshape(-1, r.shape[-1]) for r in results]
    shapes2 = [sds(r.shape, BF16) for r in flat]
    given = pl.pallas_call(
        hand_over,
        out_shape=shapes2,
        in_specs=[hb] * 5,
        out_specs=[hb] * 5,
        scratch_shapes=[pltpu.SemaphoreType.DMA((16,))],
        compiler_params=pltpu.CompilerParams(vmem_limit_bytes=4 * 1024 * 1024),
        name="hand_over",
    )(*flat)
    return tuple(g.reshape(s.shape) for g, s in zip(given, shapes))


def solution(mesh):
    return jax.shard_map(
        functools.partial(local, LAYOUT[mesh.shape["expert"]]),
        mesh=mesh,
        in_specs=(
            P(("dp", "expert"), None),
            P(("dp", "expert"), None),
            P(("dp", "expert"), None),
            P(("dp", "expert"), None),
            P("expert", "dp", None),
            P("expert", "dp", None),
            P("expert", None, "dp"),
        ),
        out_specs=(
            P(("dp", "expert"), None),
            P(("dp", "expert"), None),
            P("expert", "dp", None),
            P("expert", "dp", None),
            P("expert", None, "dp"),
        ),
        check_vma=False,
    )
```
